32 devices in a mesh: blk: 8 (over z, x), tile: 4 (over y, core).
Axes of the slice: x: 2, y: 2, z: 4, core: 2. Of those that a mesh axis runs over, the one named last changes fastest.
Arguments:
- stream_in: bfloat16 [32, 16, 16, 2240], P('tile', 'blk'), may hold values from -6 to 6
- queries: bfloat16 [32, 16, 16, 2240], P('tile', 'blk'), may hold values from -12 to 12
- key_rows: bfloat16 [32, 16, 16, 2240], P('tile', 'blk'), may hold values from -12 to 12
- value_rows: bfloat16 [32, 16, 16, 2240], P('tile', 'blk'), may hold values from -12 to 12
- w_output: bfloat16 [2240, 2240], P('tile'), may hold values from -0.125 to 0.125
- w_inner: bfloat16 [2240, 2, 4096], P(None, None, 'tile'), may hold values from -0.125 to 0.125
- w_down: bfloat16 [4096, 2240], P('tile'), may hold values from -0.09375 to 0.09375
- spatial_taps: float32 [3, 3, 2, 4096], P(None, None, None, 'tile'), may hold values from -2 to 2
- temporal_taps: float32 [3, 2, 4096], P(None, None, 'tile'), may hold values from -3.5 to 3.5
Outputs:
- layer_out: bfloat16 [32, 16, 16, 2240], P('tile', 'blk')
The draws below stay inside these ranges and needn't reach their ends.
All inputs are finite; a program needn't handle non-finite values.
Results may differ from the reference program's by a relative error of at most 0.009.
Values may be sent and summed in bfloat16 or wider, within the bound.
A program may use at most 128 MiB of HBM per device.

```python
import jax
import jax.numpy as jnp
from jax import lax

HEADS = 20
HEAD_DIM = 112
D = 2240
FF_WIN = 4096
ROWS = 32
COLS = 16
BLOCK_F = 4
TAPS = 3
FRAMES = 16


def cluster_tables(key):
    mask_key = jax.random.fold_in(key, 101)
    magnitude_key = jax.random.fold_in(key, 102)
    value_key = jax.random.fold_in(key, 103)
    active = jax.random.bernoulli(mask_key, 0.12, (HEADS, HEAD_DIM, HEAD_DIM))
    own_channel = jnp.eye(HEAD_DIM, dtype=jnp.float32)[None] > 0.5
    active = jnp.logical_or(active, own_channel)
    magnitude = jnp.exp(jax.random.uniform(magnitude_key, (HEADS, HEAD_DIM, HEAD_DIM), jnp.float32, 0.405, 1.386))
    proto_key = jnp.where(active, magnitude, 0.0)
    proto_value = 2.0 * jax.random.normal(value_key, (HEADS, HEAD_DIM, HEAD_DIM), jnp.float32)
    return (proto_key, proto_value)


def token_noise(noise_key):
    shape_heads = (ROWS, FRAMES, COLS, HEADS, HEAD_DIM)
    return jax.random.normal(noise_key, shape_heads, jnp.float32)


def pick_rows(table, clusters):
    head_index = jnp.arange(HEADS, dtype=jnp.int32)
    return table[head_index, clusters]


def positive_rows(key, salt):
    proto_key, proto_value = cluster_tables(key)
    clusters = jax.random.randint(jax.random.fold_in(key, salt), (ROWS, FRAMES, COLS, HEADS), 0, HEAD_DIM)
    gain = jnp.exp(jax.random.uniform(jax.random.fold_in(key, salt + 1), (ROWS, FRAMES, COLS, HEADS, 1), jnp.float32, -1.5, 1.5))
    noise = token_noise(jax.random.fold_in(key, salt + 2))
    rows = gain * (pick_rows(proto_key, clusters) + 0.3 * noise)
    return (rows, clusters, proto_value)


def draw_queries(key, part):
    rows, clusters, proto_value = positive_rows(key, 211)
    return jnp.clip(rows, -12.0, 12.0).reshape(ROWS, FRAMES, COLS, D).astype(jnp.bfloat16)


def draw_key_rows(key, part):
    rows, clusters, proto_value = positive_rows(key, 311)
    return jnp.clip(rows, -12.0, 12.0).reshape(ROWS, FRAMES, COLS, D).astype(jnp.bfloat16)


def draw_value_rows(key, part):
    rows, clusters, proto_value = positive_rows(key, 311)
    noise = token_noise(jax.random.fold_in(key, 411))
    offset = 2.0 * jax.random.normal(jax.random.fold_in(key, 412), (1, FRAMES, 1, HEADS, HEAD_DIM), jnp.float32)
    values = noise + pick_rows(proto_value, clusters) + offset
    return jnp.clip(values, -12.0, 12.0).reshape(ROWS, FRAMES, COLS, D).astype(jnp.bfloat16)


def level_of(rng, dims, shards, low, largest):
    def one(position, parts):
        steps = jax.random.uniform(jax.random.fold_in(jax.random.fold_in(rng, 6), position), (parts,), jnp.float32, low / len(shards), largest / len(shards))
        return jnp.repeat(jnp.exp(steps), dims[position] // parts).reshape((-1,) + (1,) * (len(dims) - position - 1))

    factor_of = one(*shards[0])
    for cut in shards[1:]:
        factor_of = factor_of * one(*cut)
    return factor_of


def gaussian(rng, shape, width, bound, cuts=(), held_as=jnp.bfloat16):
    values = jax.random.normal(rng, shape, jnp.float32) * width
    if len(cuts) > 0:
        values = level_of(rng, shape, cuts, -0.22, 0.18) * values
    return jnp.clip(values, min=-bound, max=bound).astype(held_as)


def setup_inputs(seed: int = 0) -> dict:
    key_of = jax.random.split(jax.random.key(seed), 10)
    return {
        "stream_in": gaussian(key_of[0], (ROWS, FRAMES, COLS, D), 1.0, 6.0, ((0, 4), (1, 8))),
        "queries": draw_queries(jax.random.fold_in(key_of[9], 71), 0),
        "key_rows": draw_key_rows(jax.random.fold_in(key_of[9], 71), 0),
        "value_rows": draw_value_rows(jax.random.fold_in(key_of[9], 71), 0),
        "w_output": gaussian(key_of[4], (D, D), D ** -0.5, 0.125, ((0, 4),)),
        "w_inner": gaussian(key_of[5], (D, 2, FF_WIN), D ** -0.5, 0.125, ((2, 4),)),
        "w_down": gaussian(key_of[6], (FF_WIN, D), FF_WIN ** -0.5, 0.09375, ((0, 4),)),
        "spatial_taps": gaussian(key_of[7], (3, 3, 2, FF_WIN), 9 ** -0.5, 2.0, ((3, 4),), jnp.float32),
        "temporal_taps": gaussian(key_of[8], (TAPS, 2, FF_WIN), TAPS ** -0.5, 3.5, ((2, 4),), jnp.float32),
    }


EPS = 1e-6


def spatial_conv(inner_act, spatial_taps):
    row_count = inner_act.shape[0]
    col_count = inner_act.shape[2]
    padded = jnp.pad(inner_act, ((1, 1), (0, 0), (1, 1), (0, 0), (0, 0)))
    running = jnp.zeros(inner_act.shape, jnp.float32)
    for tap_row in range(3):
        for tap_col in range(3):
            window = padded[tap_row:tap_row + row_count, :, tap_col:tap_col + col_count]
            running = running + window.astype(jnp.float32) * spatial_taps[tap_row, tap_col]
    return running


def reference(stream_in, queries, key_rows, value_rows, w_output, w_inner, w_down, spatial_taps, temporal_taps):
    highest = lax.Precision.HIGHEST
    shape_heads = (ROWS, FRAMES, COLS, HEADS, HEAD_DIM)
    query_pos = jax.nn.relu(queries.astype(jnp.float32)).reshape(shape_heads)
    key_pos = jax.nn.relu(key_rows.astype(jnp.float32)).reshape(shape_heads)
    values = value_rows.astype(jnp.float32).reshape(shape_heads)
    frame_kv = jnp.einsum('rfchd,rfche->fhde', key_pos, values, precision=highest)
    frame_z = jnp.sum(key_pos, axis=(0, 2))
    block_count = FRAMES // BLOCK_F
    block_kv = frame_kv.reshape(block_count, BLOCK_F, HEADS, HEAD_DIM, HEAD_DIM).sum(1)
    block_z = frame_z.reshape(block_count, BLOCK_F, HEADS, HEAD_DIM).sum(1)
    state = jnp.repeat(jnp.cumsum(block_kv, 0), BLOCK_F, axis=0)
    zsum = jnp.repeat(jnp.cumsum(block_z, 0), BLOCK_F, axis=0)
    numerator = jnp.einsum('rfchd,fhde->rfche', query_pos, state, precision=highest)
    denominator = jnp.einsum('rfchd,fhd->rfch', query_pos, zsum, precision=highest) + EPS
    attended = (numerator / denominator[..., None]).reshape(ROWS * FRAMES * COLS, D).astype(jnp.bfloat16)
    attn_out = jnp.dot(attended, w_output, preferred_element_type=jnp.float32)
    hidden = (stream_in.astype(jnp.float32).reshape(-1, D) + attn_out).astype(jnp.bfloat16)
    inner_act = jax.nn.silu(jnp.dot(hidden, w_inner.reshape(D, 2 * FF_WIN), preferred_element_type=jnp.float32))
    inner_act = inner_act.astype(jnp.bfloat16).reshape(ROWS, FRAMES, COLS, 2, FF_WIN)
    spatial = spatial_conv(inner_act, spatial_taps).astype(jnp.bfloat16)
    extended = jnp.pad(spatial, ((0, 0), (TAPS - 1, 0), (0, 0), (0, 0), (0, 0)))
    temporal_mix = jnp.zeros(spatial.shape, jnp.float32)
    for lag in range(TAPS):
        window = extended[:, TAPS - 1 - lag:TAPS - 1 - lag + FRAMES]
        temporal_mix = temporal_mix + window.astype(jnp.float32) * temporal_taps[lag]
    gated_out = (temporal_mix[..., 0, :] * jax.nn.silu(temporal_mix[..., 1, :])).astype(jnp.bfloat16)
    ffn_out = jnp.dot(gated_out.reshape(-1, FF_WIN), w_down, preferred_element_type=jnp.float32)
    layer_out = (hidden.astype(jnp.float32) + ffn_out).astype(jnp.bfloat16)
    return layer_out.reshape(ROWS, FRAMES, COLS, D)
```

```python
import functools

import jax
import jax.numpy as jnp
from jax import lax
from jax.experimental import pallas as pl
from jax.experimental.pallas import tpu as pltpu
from jax.sharding import PartitionSpec as P

HEADS = 20
HEAD_DIM = 112
TAPS = 3
BLOCK_F = 4
LANES = 128
EPS = 1e-06

MESH = pl.DeviceIdType.MESH


def vmem_specs(count):
    return [pl.BlockSpec(memory_space=pltpu.VMEM)] * count


def head_columns(head):
    return slice(head * HEAD_DIM, (head + 1) * HEAD_DIM)


def rows_of(i, parts, rows):
    units = -(-rows // 16)
    low, high = i * units // parts, (i + 1) * units // parts
    return slice(low * 16, min(high * 16, rows))


def front_kernel(
    dims, query_ref, key_ref, value_ref, stream_ref, w_ref, inner_ref, hidden_ref, flat_ref,
    wbuf, raw, flat, kv, got0, csum, got1, got2, total, block_send, final_send, state,
    attended, pieces, acc, local, core_s, core_r, ysend, yrecv, xsend, xrecv, csend, crecv,
    send1, recv1, send2, recv2, send3, recv3, send4, recv4,
):
    blocks, pair, ways, subs = dims
    rows = w_ref.shape[0]
    tokens, width = hidden_ref.shape
    chan = inner_ref.shape[2]
    group = pair * ways
    per_core = -(-HEADS // 2)
    per_rank = kv.shape[2]
    blk = lax.axis_index("blk")
    tile = lax.axis_index("tile")
    core = tile % 2
    y = tile // 2
    block = blk // pair
    member = blk % pair
    rank = member * ways + y
    sibling = (blk, y * 2 + 1 - core)
    ids = pair * subs

    def remote(src, dst, send, recv, device):
        return pltpu.make_async_remote_copy(
            src_ref=src, dst_ref=dst, send_sem=send, recv_sem=recv, device_id=device,
            device_id_type=MESH,
        )

    raw_copy = pltpu.make_async_copy(inner_ref, raw, local.at[0])
    own_copy = pltpu.make_async_copy(w_ref, wbuf.at[tile], local.at[1])
    raw_copy.start()
    own_copy.start()

    def peer(step):
        other = (rank + step) % group
        return other, (block * pair + other // ways, (other % ways) * 2 + core)

    def other_block(step):
        return (((block + step) % blocks) * pair + member, tile)

    barrier = pltpu.get_barrier_semaphore()
    pl.semaphore_signal(barrier, inc=1, device_id=sibling, device_id_type=MESH)
    for step in range(1, group):
        pl.semaphore_signal(barrier, inc=1, device_id=peer(step)[1], device_id_type=MESH)
    for step in range(1, blocks):
        pl.semaphore_signal(barrier, inc=1, device_id=other_block(step), device_id_type=MESH)
    pl.semaphore_wait(barrier, group + blocks - 1)

    w_core = remote(w_ref, wbuf.at[tile], core_s.at[0], core_r.at[0], sibling)
    w_core.start()

    def y_send(s, j, i):
        part = rows_of(i * subs + j, ids, rows)
        return remote(
            w_ref.at[part], wbuf.at[tile, part], ysend.at[s, j], yrecv.at[s, j],
            (blk, ((y + s) % ways) * 2 + core),
        )

    def came(s):
        return ((y + ways - s) % ways) * 2 + core

    def x_send(s, j, st, i):
        part = rows_of(i * subs + j, ids, rows)
        place = wbuf.at[came(s), part]
        return remote(
            place, place, xsend.at[st, s, j], xrecv.at[st, s, j],
            (block * pair + (member + st) % pair, tile),
        )

    def core_send(s, number):
        part = rows_of(number, ids, rows)
        place = wbuf.at[came(s), part]
        return remote(place, place, csend.at[s, number], crecv.at[s, number], sibling)

    def each_member(body):
        for i in range(pair):
            pl.when(member == i)(functools.partial(body, i))

    def start_y(j):
        def body(i):
            for s in range(1, ways):
                y_send(s, j, i).start()

        each_member(body)

    def relay_y(j):
        def body(i):
            for s in range(1, ways):
                y_send(s, j, i).wait_recv()
                for st in range(1, pair):
                    x_send(s, j, st, i).start()
                core_send(s, i * subs + j).start()

        each_member(body)

    def relay_x(j):
        def body(i):
            for s in range(1, ways):
                for st in range(1, pair):
                    source = (i + pair - st) % pair
                    x_send(s, j, st, source).wait_recv()
                    core_send(s, source * subs + j).start()

        each_member(body)

    start_y(0)

    ones = jnp.ones((tokens, LANES - HEAD_DIM), jnp.bfloat16)
    slots = group * per_rank
    for head in range(HEADS):
        keys = jnp.maximum(key_ref[:, head_columns(head)], 0)
        values = jnp.concatenate([value_ref[:, head_columns(head)], ones], axis=1)
        product = lax.dot_general(
            keys, values, (((0,), (0,)), ((), ())), preferred_element_type=jnp.float32
        )
        half, i = head // per_core, head % per_core
        kv[half, i // per_rank, i % per_rank] = product.astype(jnp.bfloat16)
    for half in range(2):
        for i in range(slots):
            if i >= per_core or half * per_core + i >= HEADS:
                kv[half, i // per_rank, i % per_rank] = jnp.zeros(kv.shape[3:], jnp.bfloat16)

    kv_core = remote(kv.at[1 - core], got0, core_s.at[1], core_r.at[1], sibling)
    kv_core.start()
    relay_y(0)
    kv_core.wait_recv()
    for r in range(group):
        csum[r] = (kv[core, r].astype(jnp.float32) + got0[r].astype(jnp.float32)).astype(
            jnp.bfloat16
        )
    first = []
    for step in range(1, group):
        other, device = peer(step)
        copy = remote(csum.at[other], got1.at[step], send1.at[step], recv1.at[step], device)
        copy.start()
        first.append(copy)
    start_y(1)
    total[...] = kv[core, rank].astype(jnp.float32) + got0[rank].astype(jnp.float32)
    for step in range(1, group):
        first[step - 1].wait_recv()
        total[...] += got1[step].astype(jnp.float32)
    block_send[...] = total[...].astype(jnp.bfloat16)

    def later(step):
        return remote(
            block_send, got2.at[step], send2.at[step], recv2.at[step], other_block(step)
        )

    for step in range(1, blocks):

        @pl.when(block + step < blocks)
        def _():
            later(step).start()

    raw_copy.wait()

    def deinterleave(start, count):
        def body(n, carry):
            where = pl.ds(pl.multiple_of(n * 64, 64), 64)
            both = raw[where]
            flat[where, 0:chan] = both[:, 0, :]
            flat[where, chan : 2 * chan] = both[:, 1, :]
            return carry

        lax.fori_loop(start, start + count, body, 0)

    steps = width // 64
    deinterleave(0, steps // 2)
    relay_y(1)
    start_y(2)
    relay_x(0)
    deinterleave(steps // 2, steps - steps // 2)
    flat_copy = pltpu.make_async_copy(flat, flat_ref, local.at[2])
    flat_copy.start()

    for step in range(1, blocks):

        @pl.when(block >= step)
        def _():
            later(step).wait_recv()
            total[...] += got2[step].astype(jnp.float32)

    final_send[...] = total[...].astype(jnp.bfloat16)
    third = []
    for step in range(1, group):
        copy = remote(
            final_send, state.at[core, rank], send3.at[step], recv3.at[step], peer(step)[1]
        )
        copy.start()
        third.append(copy)
    fourth = [remote(final_send, state.at[core, rank], send4.at[0], recv4.at[0], sibling)]
    fourth[0].start()
    state[core, rank] = total[...].astype(jnp.bfloat16)
    relay_y(2)
    start_y(3)
    relay_x(1)
    for step in range(1, group):
        third[step - 1].wait_recv()
        place = state.at[core, (rank + group - step) % group]
        copy = remote(place, place, send4.at[step], recv4.at[step], sibling)
        copy.start()
        fourth.append(copy)
    for copy in fourth:
        copy.wait_recv()

    for head in range(HEADS):
        half, i = head // per_core, head % per_core
        queries = jnp.maximum(query_ref[:, head_columns(head)], 0)
        both = jnp.dot(
            queries, state[half, i // per_rank, i % per_rank], preferred_element_type=jnp.float32
        )
        ratio = both[:, :HEAD_DIM] / (both[:, HEAD_DIM : HEAD_DIM + 1] + EPS)
        attended[:, head_columns(head)] = ratio.astype(jnp.bfloat16)
    relay_y(3)
    relay_x(2)
    for t in range(2 * ways):
        pieces[t] = attended[:, t * rows : (t + 1) * rows]

    acc[...] = stream_ref[...].astype(jnp.float32)

    def add_piece(step, carry):
        t = ((y + step // 2) % ways) * 2 + (core + step) % 2
        acc[...] += jnp.dot(pieces[t], wbuf[t], preferred_element_type=jnp.float32)
        return carry

    own_copy.wait()
    w_core.wait_recv()
    lax.fori_loop(0, 2, add_piece, 0)
    relay_x(3)
    for s in range(1, ways):
        for number in range(ids):
            core_send(s, number).wait_recv()
    lax.fori_loop(2, 2 * ways, add_piece, 0)
    hidden_ref[...] = acc[...].astype(jnp.bfloat16)

    flat_copy.wait()
    w_core.wait_send()
    kv_core.wait_send()
    for copy in first + third + fourth:
        copy.wait_send()
    for step in range(1, blocks):

        @pl.when(block + step < blocks)
        def _():
            later(step).wait_send()

    def sent(i):
        for s in range(1, ways):
            for j in range(subs):
                y_send(s, j, i).wait_send()
                for st in range(1, pair):
                    x_send(s, j, st, i).wait_send()

    each_member(sent)
    for s in range(1, ways):
        for number in range(ids):
            core_send(s, number).wait_send()


def front(query, key, value, stream, w_output, w_inner, blocks, pair, tiles):
    ways, subs = tiles // 2, 4
    group = pair * ways
    per_rank = -(-(-(-HEADS // 2)) // group)
    tokens, width = query.shape
    rows = w_output.shape[0]
    chan = w_inner.shape[2]
    bf16, f32 = jnp.bfloat16, jnp.float32
    dma = pltpu.SemaphoreType.DMA
    piece = (per_rank, HEAD_DIM, LANES)
    vmem = pltpu.VMEM
    anywhere = pl.BlockSpec(memory_space=pl.ANY)
    inside = pl.BlockSpec(memory_space=pltpu.VMEM)
    return pl.pallas_call(
        functools.partial(front_kernel, (blocks, pair, ways, subs)),
        out_shape=[
            jax.ShapeDtypeStruct((tokens, width), bf16),
            jax.ShapeDtypeStruct((width, 2 * chan), bf16),
        ],
        in_specs=[inside] * 4 + [anywhere] * 2,
        out_specs=[inside, anywhere],
        scratch_shapes=[
            vmem((tiles, rows, width), bf16),
            vmem(w_inner.shape, bf16),
            vmem((width, 2 * chan), bf16),
            vmem((2, group) + piece, bf16),
            vmem((group,) + piece, bf16),
            vmem((group,) + piece, bf16),
            vmem((group,) + piece, bf16),
            vmem((blocks,) + piece, bf16),
            vmem(piece, f32),
            vmem(piece, bf16),
            vmem(piece, bf16),
            vmem((2, group) + piece, bf16),
            vmem((tokens, width), bf16),
            vmem((tiles, tokens, rows), bf16),
            vmem((tokens, width), f32),
            dma((3,)),
            dma((2,)),
            dma((2,)),
            dma((ways, subs)),
            dma((ways, subs)),
            dma((pair, ways, subs)),
            dma((pair, ways, subs)),
            dma((ways, pair * subs)),
            dma((ways, pair * subs)),
        ]
        + [dma((group,))] * 2
        + [dma((blocks,))] * 2
        + [dma((group,))] * 4,
        compiler_params=pltpu.CompilerParams(
            collective_id=0, has_side_effects=True, vmem_limit_bytes=60 * 2**20
        ),
    )(query, key, value, stream, w_output, w_inner)


def spread_kernel(
    dims, hidden_ref, own_ref, before_ref, local, core_s, core_r, ysend, yrecv, bsend, brecv,
):
    ways, halves, blks = dims
    tokens = hidden_ref.shape[0]
    part = tokens // halves
    blk = lax.axis_index("blk")
    tile = lax.axis_index("tile")
    core = tile % 2
    y = tile // 2
    sibling = (blk, y * 2 + 1 - core)
    follower = ((blk + 1) % blks, tile)

    def remote(src, dst, send, recv, device):
        return pltpu.make_async_remote_copy(
            src_ref=src, dst_ref=dst, send_sem=send, recv_sem=recv, device_id=device,
            device_id_type=MESH,
        )

    def other(s):
        return (blk, ((y + s) % ways) * 2 + core)

    def came(s):
        return ((y + ways - s) % ways) * 2 + core

    barrier = pltpu.get_barrier_semaphore()
    pl.semaphore_signal(barrier, inc=1, device_id=sibling, device_id_type=MESH)
    for s in range(1, ways):
        pl.semaphore_signal(barrier, inc=1, device_id=other(s), device_id_type=MESH)
    pl.semaphore_signal(barrier, inc=1, device_id=follower, device_id_type=MESH)
    pl.semaphore_signal(
        barrier, inc=1, device_id=((blk + blks - 1) % blks, tile), device_id_type=MESH
    )
    pl.semaphore_wait(barrier, ways + 2)

    def rows_at(t, h):
        return pl.ds(pl.multiple_of(t * tokens + h * part, part), part)

    def piece(ref, t, h):
        return ref.at[rows_at(t, h)]

    def source(h):
        return hidden_ref.at[pl.ds(h * part, part)]

    def own_core(h):
        return remote(source(h), piece(own_ref, tile, h), core_s.at[0, 0, h], core_r.at[0, 0, h], sibling)

    def own_y(s, h):
        return remote(source(h), piece(own_ref, tile, h), ysend.at[0, s, h], yrecv.at[0, s, h], other(s))

    def own_y_core(s, h):
        place = piece(own_ref, came(s), h)
        return remote(place, place, core_s.at[0, s, h], core_r.at[0, s, h], sibling)

    def next_own(h):
        return remote(source(h), piece(before_ref, tile, h), bsend.at[0, h], brecv.at[0, h], follower)

    def next_y(s, h):
        return remote(
            piece(own_ref, came(s), h), piece(before_ref, came(s), h), bsend.at[s, h],
            brecv.at[s, h], follower,
        )

    def before_core(s, h):
        place = piece(before_ref, came(s) if s else tile, h)
        return remote(place, place, core_s.at[1, s, h], core_r.at[1, s, h], sibling)

    def before_y(s, h):
        place = piece(before_ref, tile, h)
        return remote(place, place, ysend.at[1, s, h], yrecv.at[1, s, h], other(s))

    has_next = blk + 1 < blks
    has_before = blk > 0
    by_y = range(0, halves // 2)
    by_x = range(halves // 2, halves)

    @pl.when(blk == 0)
    def _():
        before_ref[...] = jnp.zeros(before_ref.shape, jnp.bfloat16)

    mine = pltpu.make_async_copy(
        hidden_ref, own_ref.at[pl.ds(pl.multiple_of(tile * tokens, tokens), tokens)], local
    )
    mine.start()
    for h in range(halves):
        for s in range(1, ways):
            own_y(s, h).start()
    for h in range(halves):

        @pl.when(has_next)
        def _():
            next_own(h).start()

    for h in range(halves):
        own_core(h).start()

    for h in range(halves):
        for s in range(1, ways):
            own_y(s, h).wait_recv()
            own_y_core(s, h).start()
            if h in by_x:

                @pl.when(has_next)
                def _():
                    next_y(s, h).start()

        @pl.when(has_before)
        def _():
            next_own(h).wait_recv()
            before_core(0, h).start()
            if h in by_y:
                for s in range(1, ways):
                    before_y(s, h).start()

    @pl.when(has_before)
    def _():
        for s in range(1, ways):
            for h in by_y:
                before_y(s, h).wait_recv()
                before_core(s, h).start()
            for h in by_x:
                next_y(s, h).wait_recv()
                before_core(s, h).start()

    mine.wait()
    for h in range(halves):
        own_core(h).wait()
        for s in range(1, ways):
            own_y(s, h).wait_send()
            own_y_core(s, h).wait()

        @pl.when(has_next)
        def _():
            next_own(h).wait_send()
            if h in by_x:
                for s in range(1, ways):
                    next_y(s, h).wait_send()

        @pl.when(has_before)
        def _():
            for s in range(ways):
                before_core(s, h).wait()
            if h in by_y:
                for s in range(1, ways):
                    before_y(s, h).wait_send()


def spread(hidden, tiles, blks):
    ways, halves = tiles // 2, 2
    tokens, width = hidden.shape
    whole = jax.ShapeDtypeStruct((tokens * tiles, width), jnp.bfloat16)
    dma = pltpu.SemaphoreType.DMA
    return pl.pallas_call(
        functools.partial(spread_kernel, (ways, halves, blks)),
        out_shape=[whole, whole],
        in_specs=vmem_specs(1),
        out_specs=vmem_specs(2),
        scratch_shapes=[dma(())]
        + [dma((2, ways, halves))] * 4
        + [dma((ways, halves))] * 2,
        compiler_params=pltpu.CompilerParams(
            collective_id=2, has_side_effects=True, vmem_limit_bytes=32 * 2**20
        ),
    )(hidden)


def column_masks(stride, cols, width):
    col = lax.broadcasted_iota(jnp.int32, (stride, width), 0) % cols
    return col > 0, col < cols - 1


def fill_inner(hidden_ref, w_ref, inner, stride, chunk):
    tokens = hidden_ref.shape[0]
    edge = jnp.zeros((stride, inner.shape[1]), jnp.bfloat16)
    inner[:stride] = edge
    inner[stride + tokens :] = edge
    for start in range(0, tokens, chunk):
        product = jnp.dot(
            hidden_ref[start : start + chunk], w_ref[...], preferred_element_type=jnp.float32
        )
        inner[stride + start : stride + start + chunk] = jax.nn.silu(product).astype(jnp.bfloat16)


def conv_row(inner, taps_ref, row, stride, masks):
    rows = [
        inner[pl.ds(pl.multiple_of((row + a) * stride, stride), stride)].astype(jnp.float32)
        for a in range(3)
    ]
    sums = [
        sum(rows[a] * taps_ref[3 * a + b : 3 * a + b + 1] for a in range(3)) for b in range(3)
    ]
    from_left = jnp.where(masks[0], pltpu.roll(sums[0], 1, 0), 0.0)
    from_right = jnp.where(masks[1], pltpu.roll(sums[2], stride - 1, 0), 0.0)
    return sums[1] + from_left + from_right


def spatial_kernel(stride, cols, chunk, hidden_ref, w_ref, taps_ref, out_ref, inner):
    fill_inner(hidden_ref, w_ref, inner, stride, chunk)
    masks = column_masks(stride, cols, inner.shape[1])

    def body(row, carry):
        value = conv_row(inner, taps_ref, row, stride, masks)
        out_ref[pl.ds(pl.multiple_of(row * stride, stride), stride)] = value.astype(jnp.bfloat16)
        return carry

    lax.fori_loop(0, hidden_ref.shape[0] // stride, body, 0, unroll=2)


def gated_kernel(
    stride, cols, chunk, hidden_ref, wv_ref, wg_ref, sv_ref, sg_ref, tv_ref, tg_ref, ov_ref, og_ref,
    out_ref, inner_v, inner_g,
):
    fill_inner(hidden_ref, wv_ref, inner_v, stride, chunk)
    fill_inner(hidden_ref, wg_ref, inner_g, stride, chunk)
    masks = column_masks(stride, cols, inner_v.shape[1])

    def mixed(inner, taps_ref, time_ref, own_ref, row, where):
        before = conv_row(inner, taps_ref, row, stride, masks)
        before = before.astype(jnp.bfloat16).astype(jnp.float32)
        extended = jnp.concatenate([before, own_ref[where].astype(jnp.float32)], axis=0)
        total = extended[stride:] * time_ref[0:1]
        for lag in range(1, TAPS):
            start = stride - lag * cols
            total = total + extended[start : start + stride] * time_ref[lag : lag + 1]
        return total

    def body(row, carry):
        where = pl.ds(pl.multiple_of(row * stride, stride), stride)
        value = mixed(inner_v, sv_ref, tv_ref, ov_ref, row, where)
        gate = mixed(inner_g, sg_ref, tg_ref, og_ref, row, where)
        out_ref[where] = (value * jax.nn.silu(gate)).astype(jnp.bfloat16)
        return carry

    lax.fori_loop(0, hidden_ref.shape[0] // stride, body, 0)


def scatter_sum_kernel(
    rows, chunks, product_ref, hidden_ref, out_ref, got, sums, landed, send1, recv1, send2, recv2
):
    blk = lax.axis_index("blk")
    tile = lax.axis_index("tile")
    core = tile % 2
    y = tile // 2
    order = [step % rows for step in range(1, rows + 1)]

    barrier = pltpu.get_barrier_semaphore()
    pl.semaphore_signal(barrier, inc=1, device_id=(blk, y * 2 + 1 - core), device_id_type=MESH)
    for step in range(1, rows):
        pl.semaphore_signal(
            barrier, inc=1, device_id=(blk, ((y + step) % rows) * 2 + core), device_id_type=MESH
        )
    pl.semaphore_wait(barrier, rows)

    first = {}
    for step in order:
        there = (y + step) % rows
        for k in range(chunks):
            slot = step * chunks + k
            copy = pltpu.make_async_remote_copy(
                src_ref=product_ref.at[there * 2 + 1 - core, k], dst_ref=got.at[step, k],
                send_sem=send1.at[slot], recv_sem=recv1.at[slot],
                device_id=(blk, y * 2 + 1 - core), device_id_type=MESH,
            )
            copy.start()
            first[step, k] = copy
    second = {}
    for k in range(chunks):
        for step in range(1, rows):
            there = (y + step) % rows
            slot = step * chunks + k
            first[step, k].wait_recv()
            chip = product_ref[there * 2 + core, k].astype(jnp.float32) + got[step, k].astype(
                jnp.float32
            )
            sums[step, k] = chip.astype(jnp.bfloat16)
            copy = pltpu.make_async_remote_copy(
                src_ref=sums.at[step, k], dst_ref=landed.at[step, k],
                send_sem=send2.at[slot], recv_sem=recv2.at[slot],
                device_id=(blk, there * 2 + core), device_id_type=MESH,
            )
            copy.start()
            second[step, k] = copy
    for k in range(chunks):
        first[0, k].wait_recv()
        total = product_ref[tile, k].astype(jnp.float32) + got[0, k].astype(jnp.float32)
        for step in range(1, rows):
            second[step, k].wait_recv()
            total = total + landed[step, k].astype(jnp.float32)
        out_ref[k] = (hidden_ref[k].astype(jnp.float32) + total).astype(jnp.bfloat16)
    for copy in list(first.values()) + list(second.values()):
        copy.wait_send()


def scatter_sum(product, hidden, tiles):
    rows = tiles // 2
    chunks = 4
    tokens, width = hidden.shape
    piece = (chunks, tokens // chunks, width)
    bf16 = jnp.bfloat16
    sems = [pltpu.SemaphoreType.DMA((rows * chunks,))] * 4
    return pl.pallas_call(
        functools.partial(scatter_sum_kernel, rows, chunks),
        out_shape=jax.ShapeDtypeStruct(piece, bf16),
        in_specs=vmem_specs(2),
        out_specs=vmem_specs(1)[0],
        scratch_shapes=[pltpu.VMEM((rows,) + piece, bf16)] * 3 + sems,
        compiler_params=pltpu.CompilerParams(
            collective_id=1, has_side_effects=True, vmem_limit_bytes=40 * 2**20
        ),
    )(product.reshape((tiles,) + piece), hidden.reshape(piece))


def project_kernel(x_ref, w_ref, out_ref):
    product = lax.dot_general(
        x_ref[...], w_ref[...], (((1,), (1,)), ((), ())), preferred_element_type=jnp.float32
    )
    out_ref[...] = product.astype(jnp.bfloat16)


def on_device(
    stream_in, queries, key_rows, value_rows, w_output, w_inner, w_down, spatial_taps, temporal_taps
):
    row_count, frames, col_count, width = queries.shape
    tokens = row_count * frames * col_count
    tiles = lax.axis_size("tile")
    pair = BLOCK_F // frames
    blocks = lax.axis_size("blk") // pair
    bf16 = jnp.bfloat16

    flatten = lambda x: x.reshape(tokens, width)
    hidden, w_flat = front(
        flatten(queries), flatten(key_rows), flatten(value_rows), flatten(stream_in), w_output,
        w_inner, blocks, pair, tiles,
    )

    chan = w_inner.shape[2]
    space = spatial_taps.reshape(9, 2 * chan)
    time = temporal_taps.reshape(TAPS, 2 * chan)
    own_all, before_all = spread(hidden, tiles, blocks * pair)

    whole = tokens * tiles
    stride = frames * col_count
    lane_block = 256
    chunk = 256
    value_blocks = chan // lane_block
    full = lambda rows: pl.BlockSpec((rows, width), lambda j: (0, 0))
    block = lambda rows: pl.BlockSpec((rows, lane_block), lambda j: (0, j))
    gate = lambda rows: pl.BlockSpec((rows, lane_block), lambda j: (0, j + value_blocks))
    inner_scratch = pltpu.VMEM((whole + 2 * stride, lane_block), bf16)
    flops = 2 * whole * width * 2 * chan
    cost = pl.CostEstimate(
        flops=flops, bytes_accessed=2 * (whole * width + 2 * width * chan), transcendentals=0
    )
    spatial = pl.pallas_call(
        functools.partial(spatial_kernel, stride, col_count, chunk),
        grid=(2 * value_blocks,),
        out_shape=jax.ShapeDtypeStruct((whole, 2 * chan), bf16),
        in_specs=[full(whole), block(width), block(9)],
        out_specs=block(whole),
        scratch_shapes=[inner_scratch],
        cost_estimate=cost,
        compiler_params=pltpu.CompilerParams(vmem_limit_bytes=40 * 2**20),
    )(own_all, w_flat, space)
    gated_out = pl.pallas_call(
        functools.partial(gated_kernel, stride, col_count, chunk),
        grid=(value_blocks,),
        out_shape=jax.ShapeDtypeStruct((whole, chan), bf16),
        in_specs=[
            full(whole), block(width), gate(width), block(9), gate(9), block(TAPS), gate(TAPS),
            block(whole), gate(whole),
        ],
        out_specs=block(whole),
        scratch_shapes=[inner_scratch, inner_scratch],
        cost_estimate=cost,
        compiler_params=pltpu.CompilerParams(vmem_limit_bytes=48 * 2**20),
    )(before_all, w_flat, w_flat, space, space, time, time, spatial, spatial)

    product = pl.pallas_call(
        project_kernel,
        grid=(whole // chunk,),
        out_shape=jax.ShapeDtypeStruct((whole, width), bf16),
        in_specs=[
            pl.BlockSpec((chunk, chan), lambda j: (j, 0)),
            pl.BlockSpec((width, chan), lambda j: (0, 0)),
        ],
        out_specs=pl.BlockSpec((chunk, width), lambda j: (j, 0)),
        compiler_params=pltpu.CompilerParams(vmem_limit_bytes=32 * 2**20),
    )(gated_out, w_down.T)
    layer_out = scatter_sum(product, hidden, tiles)
    return layer_out.reshape(queries.shape)


def solution(mesh):
    in_specs = (
        P("tile", "blk", None, None),
        P("tile", "blk", None, None),
        P("tile", "blk", None, None),
        P("tile", "blk", None, None),
        P("tile", None),
        P(None, None, "tile"),
        P("tile", None),
        P(None, None, None, "tile"),
        P(None, None, "tile"),
    )
    out_specs = P("tile", "blk", None, None)
    return jax.shard_map(
        on_device, mesh=mesh, in_specs=in_specs, out_specs=out_specs, check_vma=False
    )
```

```python
import functools

import jax
import jax.numpy as jnp
from jax import lax
from jax.experimental import pallas as pl
from jax.experimental.pallas import tpu as pltpu
from jax.sharding import PartitionSpec as P

HEADS = 20
HEAD_DIM = 112
TAPS = 3
BLOCK_F = 4
LANES = 128
FILL = 256
EPS = 1e-06

MESH = pl.DeviceIdType.MESH


def vmem_specs(count):
    return [pl.BlockSpec(memory_space=pltpu.VMEM)] * count


def head_columns(head):
    return slice(head * HEAD_DIM, (head + 1) * HEAD_DIM)


def rows_of(i, parts, rows):
    units = -(-rows // 16)
    low, high = i * units // parts, (i + 1) * units // parts
    return slice(low * 16, min(high * 16, rows))


def front_kernel(
    dims, query_ref, key_ref, value_ref, stream_ref, w_ref, inner_ref, hidden_ref, flat_ref,
    wbuf, raw, flat, kv, got0, csum, got1, got2, total, block_send, final_send, state,
    attended, pieces, acc, local, core_s, core_r, ysend, yrecv, xsend, xrecv, csend, crecv,
    send1, recv1, send2, recv2, send3, recv3, send4, recv4,
):
    blocks, pair, ways, subs = dims
    rows = w_ref.shape[0]
    tokens, width = hidden_ref.shape
    chan = inner_ref.shape[2]
    group = pair * ways
    per_core = -(-HEADS // 2)
    per_rank = kv.shape[2]
    blk = lax.axis_index("blk")
    tile = lax.axis_index("tile")
    core = tile % 2
    y = tile // 2
    block = blk // pair
    member = blk % pair
    rank = member * ways + y
    sibling = (blk, y * 2 + 1 - core)
    ids = pair * subs

    def remote(src, dst, send, recv, device):
        return pltpu.make_async_remote_copy(
            src_ref=src, dst_ref=dst, send_sem=send, recv_sem=recv, device_id=device,
            device_id_type=MESH,
        )

    raw_copy = pltpu.make_async_copy(inner_ref, raw, local.at[0])
    own_copy = pltpu.make_async_copy(w_ref, wbuf.at[tile], local.at[1])
    raw_copy.start()
    own_copy.start()

    def peer(step):
        other = (rank + step) % group
        return other, (block * pair + other // ways, (other % ways) * 2 + core)

    def other_block(step):
        return (((block + step) % blocks) * pair + member, tile)

    barrier = pltpu.get_barrier_semaphore()
    pl.semaphore_signal(barrier, inc=1, device_id=sibling, device_id_type=MESH)
    for step in range(1, group):
        pl.semaphore_signal(barrier, inc=1, device_id=peer(step)[1], device_id_type=MESH)
    for step in range(1, blocks):
        pl.semaphore_signal(barrier, inc=1, device_id=other_block(step), device_id_type=MESH)
    pl.semaphore_wait(barrier, group + blocks - 1)

    w_core = remote(w_ref, wbuf.at[tile], core_s.at[0], core_r.at[0], sibling)
    w_core.start()

    def y_send(s, j, i):
        part = rows_of(i * subs + j, ids, rows)
        return remote(
            w_ref.at[part], wbuf.at[tile, part], ysend.at[s, j], yrecv.at[s, j],
            (blk, ((y + s) % ways) * 2 + core),
        )

    def came(s):
        return ((y + ways - s) % ways) * 2 + core

    def x_send(s, j, st, i):
        part = rows_of(i * subs + j, ids, rows)
        place = wbuf.at[came(s), part]
        return remote(
            place, place, xsend.at[st, s, j], xrecv.at[st, s, j],
            (block * pair + (member + st) % pair, tile),
        )

    def core_send(s, number):
        part = rows_of(number, ids, rows)
        place = wbuf.at[came(s), part]
        return remote(place, place, csend.at[s, number], crecv.at[s, number], sibling)

    def each_member(body):
        for i in range(pair):
            pl.when(member == i)(functools.partial(body, i))

    def start_y(j):
        def body(i):
            for s in range(1, ways):
                y_send(s, j, i).start()

        each_member(body)

    def relay_y(j):
        def body(i):
            for s in range(1, ways):
                y_send(s, j, i).wait_recv()
                for st in range(1, pair):
                    x_send(s, j, st, i).start()
                core_send(s, i * subs + j).start()

        each_member(body)

    def relay_x(j):
        def body(i):
            for s in range(1, ways):
                for st in range(1, pair):
                    source = (i + pair - st) % pair
                    x_send(s, j, st, source).wait_recv()
                    core_send(s, source * subs + j).start()

        each_member(body)

    start_y(0)

    ones = jnp.ones((tokens, LANES - HEAD_DIM), jnp.bfloat16)
    slots = group * per_rank
    for head in range(HEADS):
        keys = jnp.maximum(key_ref[:, head_columns(head)], 0)
        values = jnp.concatenate([value_ref[:, head_columns(head)], ones], axis=1)
        product = lax.dot_general(
            keys, values, (((0,), (0,)), ((), ())), preferred_element_type=jnp.float32
        )
        half, i = head // per_core, head % per_core
        kv[half, i // per_rank, i % per_rank] = product.astype(jnp.bfloat16)
    for half in range(2):
        for i in range(slots):
            if i >= per_core or half * per_core + i >= HEADS:
                kv[half, i // per_rank, i % per_rank] = jnp.zeros(kv.shape[3:], jnp.bfloat16)

    kv_core = remote(kv.at[1 - core], got0, core_s.at[1], core_r.at[1], sibling)
    kv_core.start()
    relay_y(0)
    kv_core.wait_recv()
    for r in range(group):
        csum[r] = (kv[core, r].astype(jnp.float32) + got0[r].astype(jnp.float32)).astype(
            jnp.bfloat16
        )
    first = []
    for step in range(1, group):
        other, device = peer(step)
        copy = remote(csum.at[other], got1.at[step], send1.at[step], recv1.at[step], device)
        copy.start()
        first.append(copy)
    start_y(1)
    total[...] = kv[core, rank].astype(jnp.float32) + got0[rank].astype(jnp.float32)
    for step in range(1, group):
        first[step - 1].wait_recv()
        total[...] += got1[step].astype(jnp.float32)
    block_send[...] = total[...].astype(jnp.bfloat16)

    def later(step):
        return remote(
            block_send, got2.at[step], send2.at[step], recv2.at[step], other_block(step)
        )

    for step in range(1, blocks):

        @pl.when(block + step < blocks)
        def _():
            later(step).start()

    raw_copy.wait()

    def deinterleave(start, count):
        def body(n, carry):
            where = pl.ds(pl.multiple_of(n * 64, 64), 64)
            both = raw[where]
            flat[where, 0:chan] = both[:, 0, :]
            flat[where, chan : 2 * chan] = both[:, 1, :]
            return carry

        lax.fori_loop(start, start + count, body, 0)

    steps = width // 64
    deinterleave(0, steps // 2)
    relay_y(1)
    start_y(2)
    relay_x(0)
    deinterleave(steps // 2, steps - steps // 2)
    flat_copy = pltpu.make_async_copy(flat, flat_ref, local.at[2])
    flat_copy.start()

    for step in range(1, blocks):

        @pl.when(block >= step)
        def _():
            later(step).wait_recv()
            total[...] += got2[step].astype(jnp.float32)

    final_send[...] = total[...].astype(jnp.bfloat16)
    third = []
    for step in range(1, group):
        copy = remote(
            final_send, state.at[core, rank], send3.at[step], recv3.at[step], peer(step)[1]
        )
        copy.start()
        third.append(copy)
    fourth = [remote(final_send, state.at[core, rank], send4.at[0], recv4.at[0], sibling)]
    fourth[0].start()
    state[core, rank] = total[...].astype(jnp.bfloat16)
    relay_y(2)
    start_y(3)
    relay_x(1)
    for step in range(1, group):
        third[step - 1].wait_recv()
        place = state.at[core, (rank + group - step) % group]
        copy = remote(place, place, send4.at[step], recv4.at[step], sibling)
        copy.start()
        fourth.append(copy)
    for copy in fourth:
        copy.wait_recv()

    for head in range(HEADS):
        half, i = head // per_core, head % per_core
        queries = jnp.maximum(query_ref[:, head_columns(head)], 0)
        both = jnp.dot(
            queries, state[half, i // per_rank, i % per_rank], preferred_element_type=jnp.float32
        )
        ratio = both[:, :HEAD_DIM] / (both[:, HEAD_DIM : HEAD_DIM + 1] + EPS)
        attended[:, head_columns(head)] = ratio.astype(jnp.bfloat16)
    relay_y(3)
    relay_x(2)
    for t in range(2 * ways):
        pieces[t] = attended[:, t * rows : (t + 1) * rows]

    acc[...] = stream_ref[...].astype(jnp.float32)

    def add_piece(step, carry):
        t = ((y + step // 2) % ways) * 2 + (core + step) % 2
        acc[...] += jnp.dot(pieces[t], wbuf[t], preferred_element_type=jnp.float32)
        return carry

    own_copy.wait()
    w_core.wait_recv()
    lax.fori_loop(0, 2, add_piece, 0)
    relay_x(3)
    for s in range(1, ways):
        for number in range(ids):
            core_send(s, number).wait_recv()
    lax.fori_loop(2, 2 * ways, add_piece, 0)
    hidden_ref[...] = acc[...].astype(jnp.bfloat16)

    flat_copy.wait()
    w_core.wait_send()
    kv_core.wait_send()
    for copy in first + third + fourth:
        copy.wait_send()
    for step in range(1, blocks):

        @pl.when(block + step < blocks)
        def _():
            later(step).wait_send()

    def sent(i):
        for s in range(1, ways):
            for j in range(subs):
                y_send(s, j, i).wait_send()
                for st in range(1, pair):
                    x_send(s, j, st, i).wait_send()

    each_member(sent)
    for s in range(1, ways):
        for number in range(ids):
            core_send(s, number).wait_send()


def front(query, key, value, stream, w_output, w_inner, blocks, pair, tiles):
    ways, subs = tiles // 2, 4
    group = pair * ways
    per_rank = -(-(-(-HEADS // 2)) // group)
    tokens, width = query.shape
    rows = w_output.shape[0]
    chan = w_inner.shape[2]
    bf16, f32 = jnp.bfloat16, jnp.float32
    dma = pltpu.SemaphoreType.DMA
    piece = (per_rank, HEAD_DIM, LANES)
    vmem = pltpu.VMEM
    anywhere = pl.BlockSpec(memory_space=pl.ANY)
    inside = pl.BlockSpec(memory_space=pltpu.VMEM)
    return pl.pallas_call(
        functools.partial(front_kernel, (blocks, pair, ways, subs)),
        out_shape=[
            jax.ShapeDtypeStruct((tokens, width), bf16),
            jax.ShapeDtypeStruct((width, 2 * chan), bf16),
        ],
        in_specs=[inside] * 4 + [anywhere] * 2,
        out_specs=[inside, anywhere],
        scratch_shapes=[
            vmem((tiles, rows, width), bf16),
            vmem(w_inner.shape, bf16),
            vmem((width, 2 * chan), bf16),
            vmem((2, group) + piece, bf16),
            vmem((group,) + piece, bf16),
            vmem((group,) + piece, bf16),
            vmem((group,) + piece, bf16),
            vmem((blocks,) + piece, bf16),
            vmem(piece, f32),
            vmem(piece, bf16),
            vmem(piece, bf16),
            vmem((2, group) + piece, bf16),
            vmem((tokens, width), bf16),
            vmem((tiles, tokens, rows), bf16),
            vmem((tokens, width), f32),
            dma((3,)),
            dma((2,)),
            dma((2,)),
            dma((ways, subs)),
            dma((ways, subs)),
            dma((pair, ways, subs)),
            dma((pair, ways, subs)),
            dma((ways, pair * subs)),
            dma((ways, pair * subs)),
        ]
        + [dma((group,))] * 2
        + [dma((blocks,))] * 2
        + [dma((group,))] * 4,
        compiler_params=pltpu.CompilerParams(
            collective_id=0, has_side_effects=True, vmem_limit_bytes=60 * 2**20
        ),
    )(query, key, value, stream, w_output, w_inner)


def layer_kernel(
    dims, hidden_ref, flat_ref, down_ref, space_ref, time_ref, out_ref, hid, flat, down, inner,
    gated, product, got, sums, landed, local, core_s, core_r, ysend, yrecv, bsend, brecv, psend,
    precv, rsend, rrecv,
):
    ways, halves, blks, stride, cols = dims
    tokens, width = hidden_ref.shape
    tiles = 2 * ways
    count = tokens // stride
    chan = gated.shape[1]
    part = tokens // halves
    bf16, f32 = jnp.bfloat16, jnp.float32
    blk = lax.axis_index("blk")
    tile = lax.axis_index("tile")
    core = tile % 2
    y = tile // 2
    sibling = (blk, y * 2 + 1 - core)
    follower = ((blk + 1) % blks, tile)

    def remote(src, dst, send, recv, device):
        return pltpu.make_async_remote_copy(
            src_ref=src, dst_ref=dst, send_sem=send, recv_sem=recv, device_id=device,
            device_id_type=MESH,
        )

    def lanes_at(c):
        return pl.ds(pl.multiple_of(c * FILL, FILL), FILL)

    def flat_copy(c):
        return pltpu.make_async_copy(
            flat_ref.at[:, lanes_at(c)], flat.at[:, lanes_at(c)], local.at[c + 1]
        )

    fills = 2 * chan // FILL
    for c in range(fills):
        flat_copy(c).start()
    down_copy = pltpu.make_async_copy(down_ref, down, local.at[0])
    down_copy.start()

    def there(s):
        return (y + s) % ways

    def came(s):
        return ((y + ways - s) % ways) * 2 + core

    barrier = pltpu.get_barrier_semaphore()
    pl.semaphore_signal(barrier, inc=1, device_id=sibling, device_id_type=MESH)
    for s in range(1, ways):
        pl.semaphore_signal(
            barrier, inc=1, device_id=(blk, there(s) * 2 + core), device_id_type=MESH
        )
    pl.semaphore_signal(barrier, inc=1, device_id=follower, device_id_type=MESH)
    pl.semaphore_signal(
        barrier, inc=1, device_id=((blk + blks - 1) % blks, tile), device_id_type=MESH
    )
    pl.semaphore_wait(barrier, ways + 2)

    def piece(which, t, h):
        return hid.at[which, t, pl.ds(h * part, part)]

    def source(h):
        return hidden_ref.at[pl.ds(h * part, part)]

    def own_core(h):
        return remote(
            source(h), piece(0, tile, h), core_s.at[0, 0, h], core_r.at[0, 0, h], sibling
        )

    def own_y(s, h):
        return remote(
            source(h), piece(0, tile, h), ysend.at[0, s, h], yrecv.at[0, s, h],
            (blk, there(s) * 2 + core),
        )

    def own_y_core(s, h):
        place = piece(0, came(s), h)
        return remote(place, place, core_s.at[0, s, h], core_r.at[0, s, h], sibling)

    def next_own(h):
        return remote(source(h), piece(1, tile, h), bsend.at[0, h], brecv.at[0, h], follower)

    def next_y(s, h):
        return remote(
            piece(0, came(s), h), piece(1, came(s), h), bsend.at[s, h], brecv.at[s, h], follower
        )

    def before_core(s, h):
        place = piece(1, came(s), h)
        return remote(place, place, core_s.at[1, s, h], core_r.at[1, s, h], sibling)

    def before_y(s, h):
        place = piece(1, tile, h)
        return remote(
            place, place, ysend.at[1, s, h], yrecv.at[1, s, h], (blk, there(s) * 2 + core)
        )

    def to_core(s, t):
        return remote(product.at[t], got.at[s], psend.at[s], precv.at[s], sibling)

    def to_y(s):
        return remote(
            sums.at[s], landed.at[s], rsend.at[s], rrecv.at[s], (blk, there(s) * 2 + core)
        )

    has_next = blk + 1 < blks
    has_before = blk > 0
    by_y = range(0, halves // 2)
    others = range(1, ways)
    every = range(halves)

    @pl.when(core == 0)
    def _():
        for h in every:
            for s in others:
                own_y(s, h).start()

    @pl.when(jnp.logical_and(core == 1, has_next))
    def _():
        for h in every:
            next_own(h).start()

    for h in every:
        own_core(h).start()

    edge = jnp.zeros((stride, 2 * chan), bf16)
    for which in range(2):
        inner[which, 0:stride] = edge
        inner[which, stride + tiles * tokens : 2 * stride + tiles * tokens] = edge

    @pl.when(blk == 0)
    def _():
        for t in range(tiles):
            hid[1, t] = jnp.zeros((tokens, width), bf16)

    def fill(load, which, t, first=False):
        start = pl.multiple_of((t * count + 1) * stride, stride)

        def body(c, carry):
            if first:
                flat_copy(c).wait()
            result = jnp.dot(load(), flat[:, lanes_at(c)], preferred_element_type=f32)
            inner[which, pl.ds(start, tokens), lanes_at(c)] = jax.nn.silu(result).astype(bf16)
            return carry

        lax.fori_loop(0, fills, body, 0)

    def fill_from(which, t):
        fill(lambda: hid[which, t], which, t)

    fill(lambda: hidden_ref[...], 0, tile, True)
    for h in every:
        own_core(h).wait_recv()
    fill_from(0, y * 2 + 1 - core)

    def take_own():
        for h in every:
            for s in others:
                own_y(s, h).wait_recv()
                own_y_core(s, h).start()
                if h not in by_y:
                    pl.when(has_next)(next_y(s, h).start)

    def take_before():
        @pl.when(has_before)
        def _():
            for h in every:
                next_own(h).wait_recv()
                before_core(0, h).start()
                if h in by_y:
                    for s in others:
                        before_y(s, h).start()

    def forwarded_own():
        for h in every:
            for s in others:
                own_y_core(s, h).wait_recv()

    def forwarded_before():
        @pl.when(has_before)
        def _():
            for h in every:
                before_core(0, h).wait_recv()

    @pl.when(core == 0)
    def _():
        @pl.when(has_next)
        def _():
            for h in every:
                next_own(h).start()

        take_own()

    @pl.when(core == 1)
    def _():
        for h in every:
            for s in others:
                own_y(s, h).start()
        take_before()

    pl.when(core == 0)(forwarded_before)
    pl.when(core == 1)(forwarded_own)
    for s in others:
        fill_from(0, there(s) * 2)
    fill_from(1, y * 2 + 1)

    @pl.when(core == 0)
    def _():
        take_before()
        forwarded_own()

    @pl.when(core == 1)
    def _():
        take_own()
        forwarded_before()

    fill_from(1, y * 2)
    for s in others:
        fill_from(0, there(s) * 2 + 1)

    col = lax.broadcasted_iota(jnp.int32, (stride, LANES), 0) % cols
    masks = (col > 0, col < cols - 1)

    def mix(t):
        base = t * count

        def body(c, carry):
            def mixed(lanes):
                taps = [space_ref[k : k + 1, lanes] for k in range(9)]
                times = [time_ref[k : k + 1, lanes] for k in range(TAPS)]

                def spatial(which, row):
                    loads = [
                        inner[
                            which, pl.ds(pl.multiple_of((base + row + a) * stride, stride), stride),
                            lanes,
                        ].astype(f32)
                        for a in range(3)
                    ]
                    parts = [
                        sum(loads[a] * taps[3 * a + b] for a in range(3)) for b in range(3)
                    ]
                    left = jnp.where(masks[0], pltpu.roll(parts[0], 1, 0), 0.0)
                    right = jnp.where(masks[1], pltpu.roll(parts[2], stride - 1, 0), 0.0)
                    return (parts[1] + left + right).astype(bf16).astype(f32)

                def over_time(row):
                    long = jnp.concatenate([spatial(1, row), spatial(0, row)], axis=0)
                    mixed_row = long[stride:] * times[0]
                    for lag in range(1, TAPS):
                        start = stride - lag * cols
                        mixed_row = mixed_row + long[start : start + stride] * times[lag]
                    return mixed_row

                return over_time

            value = mixed(pl.ds(pl.multiple_of(c * LANES, LANES), LANES))
            gate = mixed(pl.ds(pl.multiple_of(chan + c * LANES, LANES), LANES))
            for row in range(count):
                gated[row * stride : (row + 1) * stride, pl.ds(pl.multiple_of(c * LANES, LANES), LANES)] = (
                    value(row) * jax.nn.silu(gate(row))
                ).astype(bf16)
            return carry

        lax.fori_loop(0, chan // LANES, body, 0)
        result = lax.dot_general(
            gated[...], down[...], (((1,), (1,)), ((), ())), preferred_element_type=f32
        )
        product[t] = result.astype(bf16)

    def own_rows(t):
        mix(t)
        pl.when(core != t % 2)(to_core(0, t).start)

    down_copy.wait()
    early = [y * (tiles - 1)] if ways == 2 else []
    late = [1 + y] if ways == 2 else [y * 2, y * 2 + 1]
    for t in early:
        own_rows(t)

    @pl.when(has_before)
    def _():
        for s in others:
            for h in every:
                if h in by_y:
                    before_y(s, h).wait_recv()
                else:
                    next_y(s, h).wait_recv()
                before_core(s, h).start()

    for s in others:
        fill_from(1, there(s) * 2 + core)

    @pl.when(has_before)
    def _():
        for s in others:
            for h in every:
                before_core(s, h).wait_recv()

    for s in others:
        fill_from(1, there(s) * 2 + 1 - core)

    for s in others:
        for c in range(2):
            t = there(s) * 2 + c
            mix(t)
            pl.when(core != c)(to_core(s, t).start)

            @pl.when(core == c)
            def _():
                to_core(s, t).wait_recv()
                sums[s] = (product[t].astype(f32) + got[s].astype(f32)).astype(bf16)
                to_y(s).start()

    for t in late:
        own_rows(t)
    to_core(0, tile).wait_recv()
    for s in others:
        to_y(s).wait_recv()
    for start in range(0, tokens, stride):
        where = slice(start, start + stride)
        total = product[tile, where].astype(f32) + got[0, where].astype(f32)
        for s in others:
            total = total + landed[s, where].astype(f32)
        out_ref[where] = (hidden_ref[where].astype(f32) + total).astype(bf16)

    for h in every:
        own_core(h).wait_send()
        for s in others:
            own_y(s, h).wait_send()
            own_y_core(s, h).wait_send()

        @pl.when(has_next)
        def _():
            next_own(h).wait_send()
            if h not in by_y:
                for s in others:
                    next_y(s, h).wait_send()

        @pl.when(has_before)
        def _():
            for s in range(ways):
                before_core(s, h).wait_send()
            if h in by_y:
                for s in others:
                    before_y(s, h).wait_send()

    for s in range(ways):
        to_core(s, tile).wait_send()
    for s in others:
        to_y(s).wait_send()


def finish(hidden, flat, down, space, time, tiles, blks, stride, cols):
    ways, halves = tiles // 2, 2
    tokens, width = hidden.shape
    chan = flat.shape[1] // 2
    bf16 = jnp.bfloat16
    dma = pltpu.SemaphoreType.DMA
    vmem = pltpu.VMEM
    piece = (tokens, width)
    inside = pl.BlockSpec(memory_space=pltpu.VMEM)
    anywhere = pl.BlockSpec(memory_space=pl.ANY)
    return pl.pallas_call(
        functools.partial(layer_kernel, (ways, halves, blks, stride, cols)),
        out_shape=jax.ShapeDtypeStruct(piece, bf16),
        in_specs=[inside, anywhere, anywhere, inside, inside],
        out_specs=inside,
        scratch_shapes=[
            vmem((2, tiles) + piece, bf16),
            vmem(flat.shape, bf16),
            vmem(down.shape, bf16),
            vmem((2, tiles * tokens + 2 * stride, 2 * chan), bf16),
            vmem((tokens, chan), bf16),
            vmem((tiles,) + piece, bf16),
            vmem((ways,) + piece, bf16),
            vmem((ways,) + piece, bf16),
            vmem((ways,) + piece, bf16),
            dma((1 + 2 * chan // FILL,)),
        ]
        + [dma((2, ways, halves))] * 4
        + [dma((ways, halves))] * 2
        + [dma((ways,))] * 4,
        compiler_params=pltpu.CompilerParams(
            collective_id=1, has_side_effects=True, vmem_limit_bytes=61 * 2**20
        ),
    )(hidden, flat, down, space, time)


def on_device(
    stream_in, queries, key_rows, value_rows, w_output, w_inner, w_down, spatial_taps, temporal_taps
):
    row_count, frames, col_count, width = queries.shape
    tokens = row_count * frames * col_count
    tiles = lax.axis_size("tile")
    pair = BLOCK_F // frames
    blocks = lax.axis_size("blk") // pair
    bf16 = jnp.bfloat16

    flatten = lambda x: x.reshape(tokens, width)
    hidden, w_flat = front(
        flatten(queries), flatten(key_rows), flatten(value_rows), flatten(stream_in), w_output,
        w_inner, blocks, pair, tiles,
    )

    chan = w_inner.shape[2]
    space = spatial_taps.reshape(9, 2 * chan)
    time = temporal_taps.reshape(TAPS, 2 * chan)
    layer_out = finish(
        hidden, w_flat, w_down.T, space, time, tiles, blocks * pair, frames * col_count, col_count
    )
    return layer_out.reshape(queries.shape)


def solution(mesh):
    in_specs = (
        P("tile", "blk", None, None),
        P("tile", "blk", None, None),
        P("tile", "blk", None, None),
        P("tile", "blk", None, None),
        P("tile", None),
        P(None, None, "tile"),
        P("tile", None),
        P(None, None, None, "tile"),
        P(None, None, "tile"),
    )
    out_specs = P("tile", "blk", None, None)
    return jax.shard_map(
        on_device, mesh=mesh, in_specs=in_specs, out_specs=out_specs, check_vma=False
    )
```

```python
import functools

import jax
import jax.numpy as jnp
from jax import lax
from jax.experimental import pallas as pl
from jax.experimental.pallas import tpu as pltpu
from jax.sharding import PartitionSpec as P

HEADS = 20
HEAD_DIM = 112
TAPS = 3
BLOCK_F = 4
LANES = 128
FILL = 256
EPS = 1e-06

MESH = pl.DeviceIdType.MESH


def vmem_specs(count):
    return [pl.BlockSpec(memory_space=pltpu.VMEM)] * count


def head_columns(head):
    return slice(head * HEAD_DIM, (head + 1) * HEAD_DIM)


def rows_of(i, parts, rows):
    units = -(-rows // 16)
    low, high = i * units // parts, (i + 1) * units // parts
    return slice(low * 16, min(high * 16, rows))


def front_kernel(
    dims, query_ref, key_ref, value_ref, stream_ref, w_ref, inner_ref, hidden_ref, flat_ref,
    wbuf, raw, flat, kv, got0, csum, got1, got2, total, block_send, final_send, state,
    attended, pieces, acc, local, core_s, core_r, ysend, yrecv, xsend, xrecv, csend, crecv,
    send1, recv1, send2, recv2, send3, recv3, send4, recv4,
):
    blocks, pair, ways, subs = dims
    rows = w_ref.shape[0]
    tokens, width = hidden_ref.shape
    chan = inner_ref.shape[2]
    group = pair * ways
    per_core = -(-HEADS // 2)
    per_rank = kv.shape[2]
    blk = lax.axis_index("blk")
    tile = lax.axis_index("tile")
    core = tile % 2
    y = tile // 2
    block = blk // pair
    member = blk % pair
    rank = member * ways + y
    sibling = (blk, y * 2 + 1 - core)
    assert pair == 2 and blocks % 2 == 0
    ids = 4 * subs
    quarter = member * 2 + block % 2
    beside = (block * pair + 1 - member, tile)
    across = ((block + 1 - 2 * (block % 2)) * pair + member, tile)

    def remote(src, dst, send, recv, device):
        return pltpu.make_async_remote_copy(
            src_ref=src, dst_ref=dst, send_sem=send, recv_sem=recv, device_id=device,
            device_id_type=MESH,
        )

    raw_copy = pltpu.make_async_copy(inner_ref, raw, local.at[0])
    own_copy = pltpu.make_async_copy(w_ref, wbuf.at[tile], local.at[1])
    raw_copy.start()
    own_copy.start()

    def peer(step):
        other = (rank + step) % group
        return other, (block * pair + other // ways, (other % ways) * 2 + core)

    def other_block(step):
        return (((block + step) % blocks) * pair + member, tile)

    barrier = pltpu.get_barrier_semaphore()
    pl.semaphore_signal(barrier, inc=1, device_id=sibling, device_id_type=MESH)
    for step in range(1, group):
        pl.semaphore_signal(barrier, inc=1, device_id=peer(step)[1], device_id_type=MESH)
    for step in range(1, blocks):
        pl.semaphore_signal(barrier, inc=1, device_id=other_block(step), device_id_type=MESH)
    pl.semaphore_wait(barrier, group + blocks - 1)

    w_core = remote(w_ref, wbuf.at[tile], core_s.at[0], core_r.at[0], sibling)
    w_core.start()

    def y_send(s, j, i):
        part = rows_of(i * subs + j, ids, rows)
        return remote(
            w_ref.at[part], wbuf.at[tile, part], ysend.at[s, j], yrecv.at[s, j],
            (blk, ((y + s) % ways) * 2 + core),
        )

    def came(s):
        return ((y + ways - s) % ways) * 2 + core

    def side_send(way, s, j, i):
        part = rows_of(i * subs + j % subs, ids, rows)
        place = wbuf.at[came(s), part]
        return remote(
            place, place, xsend.at[way, s, j], xrecv.at[way, s, j], across if way else beside
        )

    def core_send(s, number):
        part = rows_of(number, ids, rows)
        place = wbuf.at[came(s), part]
        return remote(place, place, csend.at[s, number], crecv.at[s, number], sibling)

    def each_quarter(body):
        for i in range(4):
            pl.when(quarter == i)(functools.partial(body, i))

    def start_y(j):
        def body(i):
            for s in range(1, ways):
                y_send(s, j, i).start()

        each_quarter(body)

    def relay_y(j):
        def body(i):
            for s in range(1, ways):
                y_send(s, j, i).wait_recv()
                for way in range(2):
                    side_send(way, s, j, i).start()
                core_send(s, i * subs + j).start()

        each_quarter(body)

    def relay_side(j):
        def body(i):
            sources = (i ^ 2, i ^ 1)
            for s in range(1, ways):
                for way in range(2):
                    source = sources[way]
                    side_send(way, s, j, source).wait_recv()
                    if way != j % 2:
                        side_send(1 - way, s, subs + j, source).start()
                    core_send(s, source * subs + j).start()

        each_quarter(body)

    def relay_last(j):
        def body(i):
            for s in range(1, ways):
                side_send(j % 2, s, subs + j, i ^ 3).wait_recv()
                core_send(s, (i ^ 3) * subs + j).start()

        each_quarter(body)

    start_y(0)

    rows_in, steps = 64, width // 64
    place_of = lax.broadcasted_iota(jnp.int32, (rows_in, 2 * rows_in), 0) * 2
    here = lax.broadcasted_iota(jnp.int32, (rows_in, 2 * rows_in), 1)
    picks = [(here == place_of + kind).astype(jnp.bfloat16) for kind in range(2)]

    def deinterleave(start, count):
        def body(n, carry):
            where = pl.ds(pl.multiple_of(n * rows_in, rows_in), rows_in)
            both = raw[where].reshape(2 * rows_in, chan)
            for kind in range(2):
                picked = jnp.dot(picks[kind], both, preferred_element_type=jnp.float32)
                flat[where, kind * chan : (kind + 1) * chan] = picked.astype(jnp.bfloat16)
            return carry

        lax.fori_loop(start, start + count, body, 0)

    ones = jnp.ones((tokens, LANES - HEAD_DIM), jnp.bfloat16)
    slots = group * per_rank
    for head in range(HEADS):
        keys = jnp.maximum(key_ref[:, head_columns(head)], 0)
        values = jnp.concatenate([value_ref[:, head_columns(head)], ones], axis=1)
        product = lax.dot_general(
            keys, values, (((0,), (0,)), ((), ())), preferred_element_type=jnp.float32
        )
        half, i = head // per_core, head % per_core
        kv[half, i // per_rank, i % per_rank] = product.astype(jnp.bfloat16)
    for half in range(2):
        for i in range(slots):
            if i >= per_core or half * per_core + i >= HEADS:
                kv[half, i // per_rank, i % per_rank] = jnp.zeros(kv.shape[3:], jnp.bfloat16)

    kv_core = remote(kv.at[1 - core], got0, core_s.at[1], core_r.at[1], sibling)
    kv_core.start()
    raw_copy.wait()
    deinterleave(0, 4)
    kv_core.wait_recv()
    for r in range(group):
        csum[r] = (kv[core, r].astype(jnp.float32) + got0[r].astype(jnp.float32)).astype(
            jnp.bfloat16
        )
    first = []
    for step in range(1, group):
        other, device = peer(step)
        copy = remote(csum.at[other], got1.at[step], send1.at[step], recv1.at[step], device)
        copy.start()
        first.append(copy)
    start_y(1)
    deinterleave(4, 8)
    total[...] = kv[core, rank].astype(jnp.float32) + got0[rank].astype(jnp.float32)
    for step in range(1, group):
        first[step - 1].wait_recv()
        total[...] += got1[step].astype(jnp.float32)
    block_send[...] = total[...].astype(jnp.bfloat16)

    def later(step):
        return remote(
            block_send, got2.at[step], send2.at[step], recv2.at[step], other_block(step)
        )

    for step in range(1, blocks):

        @pl.when(block + step < blocks)
        def _():
            later(step).start()

    relay_y(0)
    deinterleave(12, 10)
    relay_y(1)
    deinterleave(22, 4)
    relay_side(0)

    for step in range(1, blocks):

        @pl.when(block >= step)
        def _():
            later(step).wait_recv()
            total[...] += got2[step].astype(jnp.float32)

    final_send[...] = total[...].astype(jnp.bfloat16)
    third = []
    for step in range(1, group):
        copy = remote(
            final_send, state.at[core, rank], send3.at[step], recv3.at[step], peer(step)[1]
        )
        copy.start()
        third.append(copy)
    fourth = [remote(final_send, state.at[core, rank], send4.at[0], recv4.at[0], sibling)]
    fourth[0].start()
    state[core, rank] = total[...].astype(jnp.bfloat16)
    deinterleave(26, steps - 26)
    flat_copy = pltpu.make_async_copy(flat, flat_ref, local.at[2])
    flat_copy.start()
    for step in range(1, group):
        third[step - 1].wait_recv()
        place = state.at[core, (rank + group - step) % group]
        copy = remote(place, place, send4.at[step], recv4.at[step], sibling)
        copy.start()
        fourth.append(copy)
    relay_side(1)
    for copy in fourth:
        copy.wait_recv()

    for head in range(HEADS):
        half, i = head // per_core, head % per_core
        queries = jnp.maximum(query_ref[:, head_columns(head)], 0)
        both = jnp.dot(
            queries, state[half, i // per_rank, i % per_rank], preferred_element_type=jnp.float32
        )
        ratio = both[:, :HEAD_DIM] / (both[:, HEAD_DIM : HEAD_DIM + 1] + EPS)
        attended[:, head_columns(head)] = ratio.astype(jnp.bfloat16)
    relay_last(0)
    relay_last(1)
    for t in range(2 * ways):
        pieces[t] = attended[:, t * rows : (t + 1) * rows]

    acc[...] = stream_ref[...].astype(jnp.float32)

    def add_piece(step, carry):
        t = ((y + step // 2) % ways) * 2 + (core + step) % 2
        acc[...] += jnp.dot(pieces[t], wbuf[t], preferred_element_type=jnp.float32)
        return carry

    own_copy.wait()
    w_core.wait_recv()
    lax.fori_loop(0, 2, add_piece, 0)
    for s in range(1, ways):
        for number in range(ids):
            core_send(s, number).wait_recv()
    lax.fori_loop(2, 2 * ways, add_piece, 0)
    hidden_ref[...] = acc[...].astype(jnp.bfloat16)

    flat_copy.wait()
    w_core.wait_send()
    kv_core.wait_send()
    for copy in first + third + fourth:
        copy.wait_send()
    for step in range(1, blocks):

        @pl.when(block + step < blocks)
        def _():
            later(step).wait_send()

    def sent(i):
        sources = (i ^ 2, i ^ 1)
        for s in range(1, ways):
            for j in range(subs):
                y_send(s, j, i).wait_send()
                for way in range(2):
                    side_send(way, s, j, i).wait_send()
                side_send(j % 2, s, subs + j, sources[1 - j % 2]).wait_send()

    each_quarter(sent)
    for s in range(1, ways):
        for number in range(ids):
            core_send(s, number).wait_send()


def front(query, key, value, stream, w_output, w_inner, blocks, pair, tiles):
    ways, subs = tiles // 2, 2
    group = pair * ways
    per_rank = -(-(-(-HEADS // 2)) // group)
    tokens, width = query.shape
    rows = w_output.shape[0]
    chan = w_inner.shape[2]
    bf16, f32 = jnp.bfloat16, jnp.float32
    dma = pltpu.SemaphoreType.DMA
    piece = (per_rank, HEAD_DIM, LANES)
    vmem = pltpu.VMEM
    anywhere = pl.BlockSpec(memory_space=pl.ANY)
    inside = pl.BlockSpec(memory_space=pltpu.VMEM)
    return pl.pallas_call(
        functools.partial(front_kernel, (blocks, pair, ways, subs)),
        out_shape=[
            jax.ShapeDtypeStruct((tokens, width), bf16),
            jax.ShapeDtypeStruct((width, 2 * chan), bf16),
        ],
        in_specs=[inside] * 4 + [anywhere] * 2,
        out_specs=[inside, anywhere],
        scratch_shapes=[
            vmem((tiles, rows, width), bf16),
            vmem(w_inner.shape, bf16),
            vmem((width, 2 * chan), bf16),
            vmem((2, group) + piece, bf16),
            vmem((group,) + piece, bf16),
            vmem((group,) + piece, bf16),
            vmem((group,) + piece, bf16),
            vmem((blocks,) + piece, bf16),
            vmem(piece, f32),
            vmem(piece, bf16),
            vmem(piece, bf16),
            vmem((2, group) + piece, bf16),
            vmem((tokens, width), bf16),
            vmem((tiles, tokens, rows), bf16),
            vmem((tokens, width), f32),
            dma((3,)),
            dma((2,)),
            dma((2,)),
            dma((ways, subs)),
            dma((ways, subs)),
            dma((2, ways, 2 * subs)),
            dma((2, ways, 2 * subs)),
            dma((ways, 4 * subs)),
            dma((ways, 4 * subs)),
        ]
        + [dma((group,))] * 2
        + [dma((blocks,))] * 2
        + [dma((group,))] * 4,
        compiler_params=pltpu.CompilerParams(
            collective_id=0, has_side_effects=True, vmem_limit_bytes=60 * 2**20
        ),
    )(query, key, value, stream, w_output, w_inner)


def layer_kernel(
    dims, hidden_ref, flat_ref, down_ref, space_ref, time_ref, out_ref, hid, flat, down, inner,
    gated, product, got, sums, landed, local, core_s, core_r, ysend, yrecv, bsend, brecv, psend,
    precv, rsend, rrecv,
):
    ways, halves, blks, stride, cols = dims
    tokens, width = hidden_ref.shape
    tiles = 2 * ways
    count = tokens // stride
    chan = gated.shape[1]
    part = tokens // halves
    bf16, f32 = jnp.bfloat16, jnp.float32
    blk = lax.axis_index("blk")
    tile = lax.axis_index("tile")
    core = tile % 2
    y = tile // 2
    sibling = (blk, y * 2 + 1 - core)
    follower = ((blk + 1) % blks, tile)

    def remote(src, dst, send, recv, device):
        return pltpu.make_async_remote_copy(
            src_ref=src, dst_ref=dst, send_sem=send, recv_sem=recv, device_id=device,
            device_id_type=MESH,
        )

    def lanes_at(c):
        return pl.ds(pl.multiple_of(c * FILL, FILL), FILL)

    def flat_copy(c):
        return pltpu.make_async_copy(
            flat_ref.at[:, lanes_at(c)], flat.at[:, lanes_at(c)], local.at[c + 1]
        )

    fills = 2 * chan // FILL
    for c in range(fills):
        flat_copy(c).start()
    down_copy = pltpu.make_async_copy(down_ref, down, local.at[0])
    down_copy.start()

    def there(s):
        return (y + s) % ways

    def came(s):
        return ((y + ways - s) % ways) * 2 + core

    barrier = pltpu.get_barrier_semaphore()
    pl.semaphore_signal(barrier, inc=1, device_id=sibling, device_id_type=MESH)
    for s in range(1, ways):
        pl.semaphore_signal(
            barrier, inc=1, device_id=(blk, there(s) * 2 + core), device_id_type=MESH
        )
    pl.semaphore_signal(barrier, inc=1, device_id=follower, device_id_type=MESH)
    pl.semaphore_signal(
        barrier, inc=1, device_id=((blk + blks - 1) % blks, tile), device_id_type=MESH
    )
    pl.semaphore_wait(barrier, ways + 2)

    def piece(which, t, h):
        return hid.at[which, t, pl.ds(h * part, part)]

    def source(h):
        return hidden_ref.at[pl.ds(h * part, part)]

    def own_core(h):
        return remote(
            source(h), piece(0, tile, h), core_s.at[0, 0, h], core_r.at[0, 0, h], sibling
        )

    def own_y(s, h):
        return remote(
            source(h), piece(0, tile, h), ysend.at[0, s, h], yrecv.at[0, s, h],
            (blk, there(s) * 2 + core),
        )

    def own_y_core(s, h):
        place = piece(0, came(s), h)
        return remote(place, place, core_s.at[0, s, h], core_r.at[0, s, h], sibling)

    def next_own(h):
        return remote(source(h), piece(1, tile, h), bsend.at[0, h], brecv.at[0, h], follower)

    def next_y(s, h):
        return remote(
            piece(0, came(s), h), piece(1, came(s), h), bsend.at[s, h], brecv.at[s, h], follower
        )

    def before_core(s, h):
        place = piece(1, came(s), h)
        return remote(place, place, core_s.at[1, s, h], core_r.at[1, s, h], sibling)

    def before_y(s, h):
        place = piece(1, tile, h)
        return remote(
            place, place, ysend.at[1, s, h], yrecv.at[1, s, h], (blk, there(s) * 2 + core)
        )

    def to_core(s, t):
        return remote(product.at[t], got.at[s], psend.at[s], precv.at[s], sibling)

    def to_y(s):
        return remote(
            sums.at[s], landed.at[s], rsend.at[s], rrecv.at[s], (blk, there(s) * 2 + core)
        )

    has_next = blk + 1 < blks
    has_before = blk > 0
    by_y = range(0, halves // 2)
    others = range(1, ways)
    every = range(halves)

    @pl.when(core == 0)
    def _():
        for h in every:
            for s in others:
                own_y(s, h).start()

    @pl.when(jnp.logical_and(core == 1, has_next))
    def _():
        for h in every:
            next_own(h).start()

    for h in every:
        own_core(h).start()

    edge = jnp.zeros((stride, 2 * chan), bf16)
    for which in range(2):
        inner[which, 0:stride] = edge
        inner[which, stride + tiles * tokens : 2 * stride + tiles * tokens] = edge

    @pl.when(blk == 0)
    def _():
        for t in range(tiles):
            hid[1, t] = jnp.zeros((tokens, width), bf16)

    def fill(load, which, t, first=False):
        start = pl.multiple_of((t * count + 1) * stride, stride)

        def body(c, carry):
            if first:
                flat_copy(c).wait()
            result = jnp.dot(load(), flat[:, lanes_at(c)], preferred_element_type=f32)
            inner[which, pl.ds(start, tokens), lanes_at(c)] = jax.nn.silu(result).astype(bf16)
            return carry

        lax.fori_loop(0, fills, body, 0)

    def fill_from(which, t):
        fill(lambda: hid[which, t], which, t)

    fill(lambda: hidden_ref[...], 0, tile, True)
    for h in every:
        own_core(h).wait_recv()
    fill_from(0, y * 2 + 1 - core)

    def take_own():
        for h in every:
            for s in others:
                own_y(s, h).wait_recv()
                own_y_core(s, h).start()
                if h not in by_y:
                    pl.when(has_next)(next_y(s, h).start)

    def take_before():
        @pl.when(has_before)
        def _():
            for h in every:
                next_own(h).wait_recv()
                before_core(0, h).start()
                if h in by_y:
                    for s in others:
                        before_y(s, h).start()

    def forwarded_own():
        for h in every:
            for s in others:
                own_y_core(s, h).wait_recv()

    def forwarded_before():
        @pl.when(has_before)
        def _():
            for h in every:
                before_core(0, h).wait_recv()

    @pl.when(core == 0)
    def _():
        @pl.when(has_next)
        def _():
            for h in every:
                next_own(h).start()

        take_own()

    @pl.when(core == 1)
    def _():
        for h in every:
            for s in others:
                own_y(s, h).start()
        take_before()

    pl.when(core == 0)(forwarded_before)
    pl.when(core == 1)(forwarded_own)
    for s in others:
        fill_from(0, there(s) * 2)
    fill_from(1, y * 2 + 1)

    @pl.when(core == 0)
    def _():
        take_before()
        forwarded_own()

    @pl.when(core == 1)
    def _():
        take_own()
        forwarded_before()

    fill_from(1, y * 2)
    for s in others:
        fill_from(0, there(s) * 2 + 1)

    col = lax.broadcasted_iota(jnp.int32, (stride, LANES), 0) % cols
    masks = (col > 0, col < cols - 1)

    def mix(t):
        base = t * count

        def body(c, carry):
            here = pl.ds(pl.multiple_of(c * LANES, LANES), LANES)

            def mixed(kind):
                lanes = pl.ds(pl.multiple_of(kind * chan + c * LANES, LANES), LANES)
                taps = [space_ref[k, kind : kind + 1, here] for k in range(9)]
                times = [time_ref[k, kind : kind + 1, here] for k in range(TAPS)]

                def spatial(which, row):
                    loads = [
                        inner[
                            which, pl.ds(pl.multiple_of((base + row + a) * stride, stride), stride),
                            lanes,
                        ].astype(f32)
                        for a in range(3)
                    ]
                    parts = [
                        sum(loads[a] * taps[3 * a + b] for a in range(3)) for b in range(3)
                    ]
                    left = jnp.where(masks[0], pltpu.roll(parts[0], 1, 0), 0.0)
                    right = jnp.where(masks[1], pltpu.roll(parts[2], stride - 1, 0), 0.0)
                    return (parts[1] + left + right).astype(bf16).astype(f32)

                def over_time(row):
                    long = jnp.concatenate([spatial(1, row), spatial(0, row)], axis=0)
                    mixed_row = long[stride:] * times[0]
                    for lag in range(1, TAPS):
                        start = stride - lag * cols
                        mixed_row = mixed_row + long[start : start + stride] * times[lag]
                    return mixed_row

                return over_time

            value = mixed(0)
            gate = mixed(1)
            for row in range(count):
                gated[row * stride : (row + 1) * stride, here] = (
                    value(row) * jax.nn.silu(gate(row))
                ).astype(bf16)
            return carry

        lax.fori_loop(0, chan // LANES, body, 0)
        result = lax.dot_general(
            gated[...], down[...], (((1,), (1,)), ((), ())), preferred_element_type=f32
        )
        product[t] = result.astype(bf16)

    def own_rows(t):
        mix(t)
        pl.when(core != t % 2)(to_core(0, t).start)

    down_copy.wait()
    early = [y * (tiles - 1)] if ways == 2 else []
    late = [1 + y] if ways == 2 else [y * 2, y * 2 + 1]
    for t in early:
        own_rows(t)

    @pl.when(has_before)
    def _():
        for s in others:
            for h in every:
                if h in by_y:
                    before_y(s, h).wait_recv()
                else:
                    next_y(s, h).wait_recv()
                before_core(s, h).start()

    for s in others:
        fill_from(1, there(s) * 2 + core)

    @pl.when(has_before)
    def _():
        for s in others:
            for h in every:
                before_core(s, h).wait_recv()

    for s in others:
        fill_from(1, there(s) * 2 + 1 - core)

    for s in others:
        for c in range(2):
            t = there(s) * 2 + c
            mix(t)
            pl.when(core != c)(to_core(s, t).start)

            @pl.when(core == c)
            def _():
                to_core(s, t).wait_recv()
                sums[s] = (product[t].astype(f32) + got[s].astype(f32)).astype(bf16)
                to_y(s).start()

    for t in late:
        own_rows(t)
    to_core(0, tile).wait_recv()
    for s in others:
        to_y(s).wait_recv()
    for start in range(0, tokens, stride):
        where = slice(start, start + stride)
        total = product[tile, where].astype(f32) + got[0, where].astype(f32)
        for s in others:
            total = total + landed[s, where].astype(f32)
        out_ref[where] = (hidden_ref[where].astype(f32) + total).astype(bf16)

    for h in every:
        own_core(h).wait_send()
        for s in others:
            own_y(s, h).wait_send()
            own_y_core(s, h).wait_send()

        @pl.when(has_next)
        def _():
            next_own(h).wait_send()
            if h not in by_y:
                for s in others:
                    next_y(s, h).wait_send()

        @pl.when(has_before)
        def _():
            for s in range(ways):
                before_core(s, h).wait_send()
            if h in by_y:
                for s in others:
                    before_y(s, h).wait_send()

    for s in range(ways):
        to_core(s, tile).wait_send()
    for s in others:
        to_y(s).wait_send()


def finish(hidden, flat, down, space, time, tiles, blks, stride, cols):
    ways, halves = tiles // 2, 2
    tokens, width = hidden.shape
    chan = flat.shape[1] // 2
    bf16 = jnp.bfloat16
    dma = pltpu.SemaphoreType.DMA
    vmem = pltpu.VMEM
    piece = (tokens, width)
    inside = pl.BlockSpec(memory_space=pltpu.VMEM)
    anywhere = pl.BlockSpec(memory_space=pl.ANY)
    return pl.pallas_call(
        functools.partial(layer_kernel, (ways, halves, blks, stride, cols)),
        out_shape=jax.ShapeDtypeStruct(piece, bf16),
        in_specs=[inside, anywhere, anywhere, inside, inside],
        out_specs=inside,
        scratch_shapes=[
            vmem((2, tiles) + piece, bf16),
            vmem(flat.shape, bf16),
            vmem(down.shape, bf16),
            vmem((2, tiles * tokens + 2 * stride, 2 * chan), bf16),
            vmem((tokens, chan), bf16),
            vmem((tiles,) + piece, bf16),
            vmem((ways,) + piece, bf16),
            vmem((ways,) + piece, bf16),
            vmem((ways,) + piece, bf16),
            dma((1 + 2 * chan // FILL,)),
        ]
        + [dma((2, ways, halves))] * 4
        + [dma((ways, halves))] * 2
        + [dma((ways,))] * 4,
        compiler_params=pltpu.CompilerParams(
            collective_id=1, has_side_effects=True, vmem_limit_bytes=61 * 2**20
        ),
    )(hidden, flat, down, space, time)


def on_device(
    stream_in, queries, key_rows, value_rows, w_output, w_inner, w_down, spatial_taps, temporal_taps
):
    row_count, frames, col_count, width = queries.shape
    tokens = row_count * frames * col_count
    tiles = lax.axis_size("tile")
    pair = BLOCK_F // frames
    blocks = lax.axis_size("blk") // pair
    bf16 = jnp.bfloat16

    flatten = lambda x: x.reshape(tokens, width)
    hidden, w_flat = front(
        flatten(queries), flatten(key_rows), flatten(value_rows), flatten(stream_in), w_output,
        w_inner, blocks, pair, tiles,
    )

    chan = w_inner.shape[2]
    space = spatial_taps.reshape((9,) + spatial_taps.shape[2:])
    time = temporal_taps
    layer_out = finish(
        hidden, w_flat, w_down.T, space, time, tiles, blocks * pair, frames * col_count, col_count
    )
    return layer_out.reshape(queries.shape)


def solution(mesh):
    in_specs = (
        P("tile", "blk", None, None),
        P("tile", "blk", None, None),
        P("tile", "blk", None, None),
        P("tile", "blk", None, None),
        P("tile", None),
        P(None, None, "tile"),
        P("tile", None),
        P(None, None, None, "tile"),
        P(None, None, "tile"),
    )
    out_specs = P("tile", "blk", None, None)
    return jax.shard_map(
        on_device, mesh=mesh, in_specs=in_specs, out_specs=out_specs, check_vma=False
    )
```

```python
import functools

import jax
import jax.numpy as jnp
from jax import lax
from jax.experimental import pallas as pl
from jax.experimental.pallas import tpu as pltpu
from jax.sharding import PartitionSpec as P

HEADS = 20
HEAD_DIM = 112
TAPS = 3
BLOCK_F = 4
LANES = 128
FILL = 256
EPS = 1e-06

MESH = pl.DeviceIdType.MESH


def vmem_specs(count):
    return [pl.BlockSpec(memory_space=pltpu.VMEM)] * count


def head_columns(head):
    return slice(head * HEAD_DIM, (head + 1) * HEAD_DIM)


def rows_of(i, parts, rows):
    units = -(-rows // 16)
    low, high = i * units // parts, (i + 1) * units // parts
    return slice(low * 16, min(high * 16, rows))


def front_kernel(
    dims, query_ref, key_ref, value_ref, stream_ref, w_ref, inner_ref, hidden_ref, flat_ref,
    wbuf, raw, flat, kv, got0, csum, got1, got2, total, block_send, final_send, state,
    attended, pieces, acc, local, core_s, core_r, ysend, yrecv, xsend, xrecv, csend, crecv,
    send1, recv1, send2, recv2, send3, recv3, send4, recv4,
):
    blocks, pair, ways, subs = dims
    rows = w_ref.shape[0]
    tokens, width = hidden_ref.shape
    chan = inner_ref.shape[2]
    group = pair * ways
    per_core = -(-HEADS // 2)
    per_rank = kv.shape[2]
    blk = lax.axis_index("blk")
    tile = lax.axis_index("tile")
    core = tile % 2
    y = tile // 2
    block = blk // pair
    member = blk % pair
    rank = member * ways + y
    sibling = (blk, y * 2 + 1 - core)
    assert pair == 2 and blocks % 2 == 0
    ids = 4 * subs
    quarter = member * 2 + block % 2
    beside = (block * pair + 1 - member, tile)
    across = ((block + 1 - 2 * (block % 2)) * pair + member, tile)

    def remote(src, dst, send, recv, device):
        return pltpu.make_async_remote_copy(
            src_ref=src, dst_ref=dst, send_sem=send, recv_sem=recv, device_id=device,
            device_id_type=MESH,
        )

    raw_copy = pltpu.make_async_copy(inner_ref, raw, local.at[0])
    own_copy = pltpu.make_async_copy(w_ref, wbuf.at[tile], local.at[1])
    raw_copy.start()
    own_copy.start()

    def peer(step):
        other = (rank + step) % group
        return other, (block * pair + other // ways, (other % ways) * 2 + core)

    def other_block(step):
        return (((block + step) % blocks) * pair + member, tile)

    barrier = pltpu.get_barrier_semaphore()
    pl.semaphore_signal(barrier, inc=1, device_id=sibling, device_id_type=MESH)
    for step in range(1, group):
        pl.semaphore_signal(barrier, inc=1, device_id=peer(step)[1], device_id_type=MESH)
    for step in range(1, blocks):
        pl.semaphore_signal(barrier, inc=1, device_id=other_block(step), device_id_type=MESH)
    pl.semaphore_wait(barrier, group + blocks - 1)

    w_core = remote(w_ref, wbuf.at[tile], core_s.at[0], core_r.at[0], sibling)
    w_core.start()

    def number_of(j, i):
        return i * subs + j if j < subs else (i ^ 3) * subs + j - subs

    def y_send(s, j, i):
        part = rows_of(number_of(j, i), ids, rows)
        return remote(
            w_ref.at[part], wbuf.at[tile, part], ysend.at[s, j], yrecv.at[s, j],
            (blk, ((y + s) % ways) * 2 + core),
        )

    def came(s):
        return ((y + ways - s) % ways) * 2 + core

    def side_send(way, s, j, i):
        part = rows_of(i * subs + j, ids, rows)
        place = wbuf.at[came(s), part]
        return remote(
            place, place, xsend.at[way, s, j], xrecv.at[way, s, j], across if way else beside
        )

    def core_send(s, number):
        part = rows_of(number, ids, rows)
        place = wbuf.at[came(s), part]
        return remote(place, place, csend.at[s, number], crecv.at[s, number], sibling)

    def each_quarter(body):
        for i in range(4):
            pl.when(quarter == i)(functools.partial(body, i))

    def start_y(j):
        def body(i):
            for s in range(1, ways):
                y_send(s, j, i).start()

        each_quarter(body)

    def relay_y(j):
        def body(i):
            for s in range(1, ways):
                y_send(s, j, i).wait_recv()
                if j < subs:
                    for way in range(2):
                        side_send(way, s, j, i).start()
                core_send(s, number_of(j, i)).start()

        each_quarter(body)

    def relay_side(j):
        def body(i):
            sources = (i ^ 2, i ^ 1)
            for s in range(1, ways):
                for way in range(2):
                    source = sources[way]
                    side_send(way, s, j, source).wait_recv()
                    core_send(s, source * subs + j).start()

        each_quarter(body)

    start_y(0)

    rows_in, steps = 64, width // 64
    place_of = lax.broadcasted_iota(jnp.int32, (rows_in, 2 * rows_in), 0) * 2
    here = lax.broadcasted_iota(jnp.int32, (rows_in, 2 * rows_in), 1)
    picks = [(here == place_of + kind).astype(jnp.bfloat16) for kind in range(2)]

    def deinterleave(start, count):
        def body(n, carry):
            where = pl.ds(pl.multiple_of(n * rows_in, rows_in), rows_in)
            both = raw[where].reshape(2 * rows_in, chan)
            for kind in range(2):
                picked = jnp.dot(picks[kind], both, preferred_element_type=jnp.float32)
                flat[where, kind * chan : (kind + 1) * chan] = picked.astype(jnp.bfloat16)
            return carry

        lax.fori_loop(start, start + count, body, 0)

    ones = jnp.ones((tokens, LANES - HEAD_DIM), jnp.bfloat16)
    slots = group * per_rank
    for head in range(HEADS):
        keys = jnp.maximum(key_ref[:, head_columns(head)], 0)
        values = jnp.concatenate([value_ref[:, head_columns(head)], ones], axis=1)
        product = lax.dot_general(
            keys, values, (((0,), (0,)), ((), ())), preferred_element_type=jnp.float32
        )
        half, i = head // per_core, head % per_core
        kv[half, i // per_rank, i % per_rank] = product.astype(jnp.bfloat16)
    for half in range(2):
        for i in range(slots):
            if i >= per_core or half * per_core + i >= HEADS:
                kv[half, i // per_rank, i % per_rank] = jnp.zeros(kv.shape[3:], jnp.bfloat16)

    kv_core = remote(kv.at[1 - core], got0, core_s.at[1], core_r.at[1], sibling)
    kv_core.start()
    raw_copy.wait()
    deinterleave(0, 4)
    kv_core.wait_recv()
    for r in range(group):
        csum[r] = (kv[core, r].astype(jnp.float32) + got0[r].astype(jnp.float32)).astype(
            jnp.bfloat16
        )
    first = []
    for step in range(1, group):
        other, device = peer(step)
        copy = remote(csum.at[other], got1.at[step], send1.at[step], recv1.at[step], device)
        copy.start()
        first.append(copy)
    start_y(1)
    relay_y(0)
    deinterleave(4, 8)
    total[...] = kv[core, rank].astype(jnp.float32) + got0[rank].astype(jnp.float32)
    for step in range(1, group):
        first[step - 1].wait_recv()
        total[...] += got1[step].astype(jnp.float32)
    block_send[...] = total[...].astype(jnp.bfloat16)

    def later(step):
        return remote(
            block_send, got2.at[step], send2.at[step], recv2.at[step], other_block(step)
        )

    for step in range(1, blocks):

        @pl.when(block + step < blocks)
        def _():
            later(step).start()

    start_y(2)
    deinterleave(12, 14)
    relay_y(1)
    relay_side(0)

    for step in range(1, blocks):

        @pl.when(block >= step)
        def _():
            later(step).wait_recv()
            total[...] += got2[step].astype(jnp.float32)

    final_send[...] = total[...].astype(jnp.bfloat16)
    third = []
    for step in range(1, group):
        copy = remote(
            final_send, state.at[core, rank], send3.at[step], recv3.at[step], peer(step)[1]
        )
        copy.start()
        third.append(copy)
    fourth = [remote(final_send, state.at[core, rank], send4.at[0], recv4.at[0], sibling)]
    fourth[0].start()
    start_y(3)
    state[core, rank] = total[...].astype(jnp.bfloat16)
    deinterleave(26, steps - 26)
    flat_copy = pltpu.make_async_copy(flat, flat_ref, local.at[2])
    flat_copy.start()
    for step in range(1, group):
        third[step - 1].wait_recv()
        place = state.at[core, (rank + group - step) % group]
        copy = remote(place, place, send4.at[step], recv4.at[step], sibling)
        copy.start()
        fourth.append(copy)
    for copy in fourth:
        copy.wait_recv()

    for head in range(HEADS):
        half, i = head // per_core, head % per_core
        queries = jnp.maximum(query_ref[:, head_columns(head)], 0)
        both = jnp.dot(
            queries, state[half, i // per_rank, i % per_rank], preferred_element_type=jnp.float32
        )
        ratio = both[:, :HEAD_DIM] / (both[:, HEAD_DIM : HEAD_DIM + 1] + EPS)
        attended[:, head_columns(head)] = ratio.astype(jnp.bfloat16)
    relay_y(2)
    relay_side(1)
    relay_y(3)
    for t in range(2 * ways):
        pieces[t] = attended[:, t * rows : (t + 1) * rows]

    acc[...] = stream_ref[...].astype(jnp.float32)

    def add_piece(step, carry):
        t = ((y + step // 2) % ways) * 2 + (core + step) % 2
        acc[...] += jnp.dot(pieces[t], wbuf[t], preferred_element_type=jnp.float32)
        return carry

    own_copy.wait()
    w_core.wait_recv()
    lax.fori_loop(0, 2, add_piece, 0)
    for s in range(1, ways):
        for number in range(ids):
            core_send(s, number).wait_recv()
    lax.fori_loop(2, 2 * ways, add_piece, 0)
    hidden_ref[...] = acc[...].astype(jnp.bfloat16)

    flat_copy.wait()
    w_core.wait_send()
    kv_core.wait_send()
    for copy in first + third + fourth:
        copy.wait_send()
    for step in range(1, blocks):

        @pl.when(block + step < blocks)
        def _():
            later(step).wait_send()

    def sent(i):
        for s in range(1, ways):
            for j in range(2 * subs):
                y_send(s, j, i).wait_send()
            for j in range(subs):
                for way in range(2):
                    side_send(way, s, j, i).wait_send()

    each_quarter(sent)
    for s in range(1, ways):
        for number in range(ids):
            core_send(s, number).wait_send()


def front(query, key, value, stream, w_output, w_inner, blocks, pair, tiles):
    ways, subs = tiles // 2, 2
    group = pair * ways
    per_rank = -(-(-(-HEADS // 2)) // group)
    tokens, width = query.shape
    rows = w_output.shape[0]
    chan = w_inner.shape[2]
    bf16, f32 = jnp.bfloat16, jnp.float32
    dma = pltpu.SemaphoreType.DMA
    piece = (per_rank, HEAD_DIM, LANES)
    vmem = pltpu.VMEM
    anywhere = pl.BlockSpec(memory_space=pl.ANY)
    inside = pl.BlockSpec(memory_space=pltpu.VMEM)
    return pl.pallas_call(
        functools.partial(front_kernel, (blocks, pair, ways, subs)),
        out_shape=[
            jax.ShapeDtypeStruct((tokens, width), bf16),
            jax.ShapeDtypeStruct((width, 2 * chan), bf16),
        ],
        in_specs=[inside] * 4 + [anywhere] * 2,
        out_specs=[inside, anywhere],
        scratch_shapes=[
            vmem((tiles, rows, width), bf16),
            vmem(w_inner.shape, bf16),
            vmem((width, 2 * chan), bf16),
            vmem((2, group) + piece, bf16),
            vmem((group,) + piece, bf16),
            vmem((group,) + piece, bf16),
            vmem((group,) + piece, bf16),
            vmem((blocks,) + piece, bf16),
            vmem(piece, f32),
            vmem(piece, bf16),
            vmem(piece, bf16),
            vmem((2, group) + piece, bf16),
            vmem((tokens, width), bf16),
            vmem((tiles, tokens, rows), bf16),
            vmem((tokens, width), f32),
            dma((3,)),
            dma((2,)),
            dma((2,)),
            dma((ways, 2 * subs)),
            dma((ways, 2 * subs)),
            dma((2, ways, subs)),
            dma((2, ways, subs)),
            dma((ways, 4 * subs)),
            dma((ways, 4 * subs)),
        ]
        + [dma((group,))] * 2
        + [dma((blocks,))] * 2
        + [dma((group,))] * 4,
        compiler_params=pltpu.CompilerParams(
            collective_id=0, has_side_effects=True, vmem_limit_bytes=60 * 2**20
        ),
    )(query, key, value, stream, w_output, w_inner)


def layer_kernel(
    dims, hidden_ref, flat_ref, down_ref, space_ref, time_ref, out_ref, hid, flat, down, inner,
    gated, product, got, sums, landed, local, core_s, core_r, ysend, yrecv, bsend, brecv, psend,
    precv, rsend, rrecv,
):
    ways, halves, blks, stride, cols = dims
    tokens, width = hidden_ref.shape
    tiles = 2 * ways
    count = tokens // stride
    chan = gated.shape[1]
    part = tokens // halves
    bf16, f32 = jnp.bfloat16, jnp.float32
    blk = lax.axis_index("blk")
    tile = lax.axis_index("tile")
    core = tile % 2
    y = tile // 2
    sibling = (blk, y * 2 + 1 - core)
    follower = ((blk + 1) % blks, tile)

    def remote(src, dst, send, recv, device):
        return pltpu.make_async_remote_copy(
            src_ref=src, dst_ref=dst, send_sem=send, recv_sem=recv, device_id=device,
            device_id_type=MESH,
        )

    def lanes_at(c):
        return pl.ds(pl.multiple_of(c * FILL, FILL), FILL)

    def flat_copy(c):
        return pltpu.make_async_copy(
            flat_ref.at[:, lanes_at(c)], flat.at[:, lanes_at(c)], local.at[c + 1]
        )

    fills = 2 * chan // FILL
    for c in range(fills):
        flat_copy(c).start()
    down_copy = pltpu.make_async_copy(down_ref, down, local.at[0])
    down_copy.start()

    def there(s):
        return (y + s) % ways

    def came(s):
        return ((y + ways - s) % ways) * 2 + core

    barrier = pltpu.get_barrier_semaphore()
    pl.semaphore_signal(barrier, inc=1, device_id=sibling, device_id_type=MESH)
    for s in range(1, ways):
        pl.semaphore_signal(
            barrier, inc=1, device_id=(blk, there(s) * 2 + core), device_id_type=MESH
        )
    pl.semaphore_signal(barrier, inc=1, device_id=follower, device_id_type=MESH)
    pl.semaphore_signal(
        barrier, inc=1, device_id=((blk + blks - 1) % blks, tile), device_id_type=MESH
    )
    pl.semaphore_wait(barrier, ways + 2)

    def piece(which, t, h):
        return hid.at[which, t, pl.ds(h * part, part)]

    def source(h):
        return hidden_ref.at[pl.ds(h * part, part)]

    def own_core(h):
        return remote(
            source(h), piece(0, tile, h), core_s.at[0, 0, h], core_r.at[0, 0, h], sibling
        )

    def own_y(s, h):
        return remote(
            source(h), piece(0, tile, h), ysend.at[0, s, h], yrecv.at[0, s, h],
            (blk, there(s) * 2 + core),
        )

    def own_y_core(s, h):
        place = piece(0, came(s), h)
        return remote(place, place, core_s.at[0, s, h], core_r.at[0, s, h], sibling)

    def next_own(h):
        return remote(source(h), piece(1, tile, h), bsend.at[0, h], brecv.at[0, h], follower)

    def next_y(s, h):
        return remote(
            piece(0, came(s), h), piece(1, came(s), h), bsend.at[s, h], brecv.at[s, h], follower
        )

    def before_core(s, h):
        place = piece(1, came(s), h)
        return remote(place, place, core_s.at[1, s, h], core_r.at[1, s, h], sibling)

    def before_y(s, h):
        place = piece(1, tile, h)
        return remote(
            place, place, ysend.at[1, s, h], yrecv.at[1, s, h], (blk, there(s) * 2 + core)
        )

    def half_rows(ref, s, h):
        return ref.at[s, pl.ds(h * part, part)]

    def to_core(s, t, h):
        return remote(
            half_rows(product, t, h), half_rows(got, s, h), psend.at[s, h], precv.at[s, h], sibling
        )

    def to_y(s, h):
        return remote(
            half_rows(sums, s, h), half_rows(landed, s, h), rsend.at[s, h], rrecv.at[s, h],
            (blk, there(s) * 2 + core),
        )

    has_next = blk + 1 < blks
    has_before = blk > 0
    by_y = range(0, halves // 2)
    others = range(1, ways)
    every = range(halves)

    @pl.when(core == 0)
    def _():
        for h in every:
            for s in others:
                own_y(s, h).start()

    @pl.when(jnp.logical_and(core == 1, has_next))
    def _():
        for h in every:
            next_own(h).start()

    for h in every:
        own_core(h).start()

    edge = jnp.zeros((stride, 2 * chan), bf16)
    for which in range(2):
        inner[which, 0:stride] = edge
        inner[which, stride + tiles * tokens : 2 * stride + tiles * tokens] = edge

    @pl.when(blk == 0)
    def _():
        for t in range(tiles):
            hid[1, t] = jnp.zeros((tokens, width), bf16)

    def fill(load, which, t, first=False):
        start = pl.multiple_of((t * count + 1) * stride, stride)

        def body(c, carry):
            if first:
                flat_copy(c).wait()
            result = jnp.dot(load(), flat[:, lanes_at(c)], preferred_element_type=f32)
            inner[which, pl.ds(start, tokens), lanes_at(c)] = jax.nn.silu(result).astype(bf16)
            return carry

        lax.fori_loop(0, fills, body, 0)

    def fill_from(which, t):
        fill(lambda: hid[which, t], which, t)

    fill(lambda: hidden_ref[...], 0, tile, True)
    for h in every:
        own_core(h).wait_recv()
    fill_from(0, y * 2 + 1 - core)

    def take_own():
        for h in every:
            for s in others:
                own_y(s, h).wait_recv()
                own_y_core(s, h).start()
                if h not in by_y:
                    pl.when(has_next)(next_y(s, h).start)

    def take_before():
        @pl.when(has_before)
        def _():
            for h in every:
                next_own(h).wait_recv()
                before_core(0, h).start()
                if h in by_y:
                    for s in others:
                        before_y(s, h).start()

    def forwarded_own():
        for h in every:
            for s in others:
                own_y_core(s, h).wait_recv()

    def forwarded_before():
        @pl.when(has_before)
        def _():
            for h in every:
                before_core(0, h).wait_recv()

    @pl.when(core == 0)
    def _():
        @pl.when(has_next)
        def _():
            for h in every:
                next_own(h).start()

        take_own()

    @pl.when(core == 1)
    def _():
        for h in every:
            for s in others:
                own_y(s, h).start()
        take_before()

    pl.when(core == 0)(forwarded_before)
    pl.when(core == 1)(forwarded_own)
    for s in others:
        fill_from(0, there(s) * 2)
    fill_from(1, y * 2 + 1)

    @pl.when(core == 0)
    def _():
        take_before()
        forwarded_own()

    @pl.when(core == 1)
    def _():
        take_own()
        forwarded_before()

    fill_from(1, y * 2)
    for s in others:
        fill_from(0, there(s) * 2 + 1)

    col = lax.broadcasted_iota(jnp.int32, (stride, LANES), 0) % cols
    masks = (col > 0, col < cols - 1)

    def mix(t, first, rows):
        base = t * count + first

        def body(c, carry):
            here = pl.ds(pl.multiple_of(c * LANES, LANES), LANES)

            def mixed(kind):
                lanes = pl.ds(pl.multiple_of(kind * chan + c * LANES, LANES), LANES)
                taps = [space_ref[k, kind : kind + 1, here] for k in range(9)]
                times = [time_ref[k, kind : kind + 1, here] for k in range(TAPS)]

                def spatial(which, row):
                    loads = [
                        inner[
                            which, pl.ds(pl.multiple_of((base + row + a) * stride, stride), stride),
                            lanes,
                        ].astype(f32)
                        for a in range(3)
                    ]
                    parts = [
                        sum(loads[a] * taps[3 * a + b] for a in range(3)) for b in range(3)
                    ]
                    left = jnp.where(masks[0], pltpu.roll(parts[0], 1, 0), 0.0)
                    right = jnp.where(masks[1], pltpu.roll(parts[2], stride - 1, 0), 0.0)
                    return (parts[1] + left + right).astype(bf16).astype(f32)

                def over_time(row):
                    long = jnp.concatenate([spatial(1, row), spatial(0, row)], axis=0)
                    mixed_row = long[stride:] * times[0]
                    for lag in range(1, TAPS):
                        start = stride - lag * cols
                        mixed_row = mixed_row + long[start : start + stride] * times[lag]
                    return mixed_row

                return over_time

            value = mixed(0)
            gate = mixed(1)
            for row in range(rows):
                gated[row * stride : (row + 1) * stride, here] = (
                    value(row) * jax.nn.silu(gate(row))
                ).astype(bf16)
            return carry

        lax.fori_loop(0, chan // LANES, body, 0)
        result = lax.dot_general(
            gated[: rows * stride], down[...], (((1,), (1,)), ((), ())), preferred_element_type=f32
        )
        product[t, first * stride : (first + rows) * stride] = result.astype(bf16)

    def own_rows(t):
        mix(t, 0, count)

        @pl.when(core != t % 2)
        def _():
            for h in every:
                to_core(0, t, h).start()

    down_copy.wait()
    early = [y * (tiles - 1)] if ways == 2 else []
    late = [1 + y] if ways == 2 else [y * 2, y * 2 + 1]
    for t in early:
        own_rows(t)

    @pl.when(has_before)
    def _():
        for s in others:
            for h in every:
                if h in by_y:
                    before_y(s, h).wait_recv()
                else:
                    next_y(s, h).wait_recv()
                before_core(s, h).start()

    for s in others:
        fill_from(1, there(s) * 2 + core)

    @pl.when(has_before)
    def _():
        for s in others:
            for h in every:
                before_core(s, h).wait_recv()

    for s in others:
        fill_from(1, there(s) * 2 + 1 - core)

    for s in others:
        for c in range(2):
            t = there(s) * 2 + c
            for h in every:
                mix(t, h * part // stride, part // stride)
                pl.when(core != c)(to_core(s, t, h).start)

                @pl.when(core == c)
                def _():
                    to_core(s, t, h).wait_recv()
                    where = slice(h * part, (h + 1) * part)
                    sums[s, where] = (
                        product[t, where].astype(f32) + got[s, where].astype(f32)
                    ).astype(bf16)
                    to_y(s, h).start()

    for t in late:
        own_rows(t)
    for h in every:
        to_core(0, tile, h).wait_recv()
        for s in others:
            to_y(s, h).wait_recv()
        for start in range(h * part, (h + 1) * part, stride):
            where = slice(start, start + stride)
            total = product[tile, where].astype(f32) + got[0, where].astype(f32)
            for s in others:
                total = total + landed[s, where].astype(f32)
            out_ref[where] = (hidden_ref[where].astype(f32) + total).astype(bf16)

    for h in every:
        own_core(h).wait_send()
        for s in others:
            own_y(s, h).wait_send()
            own_y_core(s, h).wait_send()

        @pl.when(has_next)
        def _():
            next_own(h).wait_send()
            if h not in by_y:
                for s in others:
                    next_y(s, h).wait_send()

        @pl.when(has_before)
        def _():
            for s in range(ways):
                before_core(s, h).wait_send()
            if h in by_y:
                for s in others:
                    before_y(s, h).wait_send()

    for h in every:
        for s in range(ways):
            to_core(s, tile, h).wait_send()
        for s in others:
            to_y(s, h).wait_send()


def finish(hidden, flat, down, space, time, tiles, blks, stride, cols):
    ways, halves = tiles // 2, 2
    tokens, width = hidden.shape
    chan = flat.shape[1] // 2
    bf16 = jnp.bfloat16
    dma = pltpu.SemaphoreType.DMA
    vmem = pltpu.VMEM
    piece = (tokens, width)
    inside = pl.BlockSpec(memory_space=pltpu.VMEM)
    anywhere = pl.BlockSpec(memory_space=pl.ANY)
    return pl.pallas_call(
        functools.partial(layer_kernel, (ways, halves, blks, stride, cols)),
        out_shape=jax.ShapeDtypeStruct(piece, bf16),
        in_specs=[inside, anywhere, anywhere, inside, inside],
        out_specs=inside,
        scratch_shapes=[
            vmem((2, tiles) + piece, bf16),
            vmem(flat.shape, bf16),
            vmem(down.shape, bf16),
            vmem((2, tiles * tokens + 2 * stride, 2 * chan), bf16),
            vmem((tokens, chan), bf16),
            vmem((tiles,) + piece, bf16),
            vmem((ways,) + piece, bf16),
            vmem((ways,) + piece, bf16),
            vmem((ways,) + piece, bf16),
            dma((1 + 2 * chan // FILL,)),
        ]
        + [dma((2, ways, halves))] * 4
        + [dma((ways, halves))] * 6,
        compiler_params=pltpu.CompilerParams(
            collective_id=1, has_side_effects=True, vmem_limit_bytes=61 * 2**20
        ),
    )(hidden, flat, down, space, time)


def on_device(
    stream_in, queries, key_rows, value_rows, w_output, w_inner, w_down, spatial_taps, temporal_taps
):
    row_count, frames, col_count, width = queries.shape
    tokens = row_count * frames * col_count
    tiles = lax.axis_size("tile")
    pair = BLOCK_F // frames
    blocks = lax.axis_size("blk") // pair
    bf16 = jnp.bfloat16

    flatten = lambda x: x.reshape(tokens, width)
    hidden, w_flat = front(
        flatten(queries), flatten(key_rows), flatten(value_rows), flatten(stream_in), w_output,
        w_inner, blocks, pair, tiles,
    )

    chan = w_inner.shape[2]
    space = spatial_taps.reshape((9,) + spatial_taps.shape[2:])
    time = temporal_taps
    layer_out = finish(
        hidden, w_flat, w_down.T, space, time, tiles, blocks * pair, frames * col_count, col_count
    )
    return layer_out.reshape(queries.shape)


def solution(mesh):
    in_specs = (
        P("tile", "blk", None, None),
        P("tile", "blk", None, None),
        P("tile", "blk", None, None),
        P("tile", "blk", None, None),
        P("tile", None),
        P(None, None, "tile"),
        P("tile", None),
        P(None, None, None, "tile"),
        P(None, None, "tile"),
    )
    out_specs = P("tile", "blk", None, None)
    return jax.shard_map(
        on_device, mesh=mesh, in_specs=in_specs, out_specs=out_specs, check_vma=False
    )
```
